512 devices in a mesh: depth: 16 (over y, core), lat: 32 (over z, x).
Axes of the slice: x: 4, y: 8, z: 8, core: 2. Of those that a mesh axis runs over, the one named last changes fastest.
Arguments:
- potential: float32 [2, 16, 2, 1024, 2048], P(None, 'depth', None, 'lat'), may hold values from -3 to 3, as said below
- incident: float32 [2, 2, 1024, 1024], P(None, None, 'lat'), may hold values from -6 to 6
- measured: float32 [2, 1024, 1024], P(None, 'lat'), may hold values from 0 to 3
- offsets: int32 [2, 2], replicated, may hold values from 0 to 1024, as said below
- kernel: bfloat16 [2, 9], replicated, may hold values from -1 to 1
Outputs:
- potential_grad: float32 [2, 16, 2, 1024, 2048], P(None, 'depth', None, 'lat')
The draws below stay inside these ranges and needn't reach their ends.
Inputs may be any that keep to these rules, and one draw needn't show every extreme that they name: Row offsets are multiples of 32 from 0 to 1024; column offsets run from 0 to 1024. `potential`: part 0 (phase) lies in -3 to 3; part 1 (absorption) lies in 0.004 to 0.05.
All inputs are finite; a program needn't handle non-finite values.
Results may differ from the reference program's by a relative error of at most 0.038.
Values may be sent and summed in bfloat16 or wider, within the bound.
No kernel may reach another device: no remote copies, remote signals or barrier semaphores. Data moves between devices by JAX's collectives and lax.ppermute only.
A program may use at most 64 MiB of HBM per device.

```python
import jax
import jax.numpy as jnp
from jax import lax

WIN = 1024
HALF = 4
PROBES = 2
COL_SCAN = 1024
BAND = 32
SLICES = 16
OBJ_COLS = 2048


def draw_potential(key, part):
    phase_key, absorb_key = jax.random.split(key)
    shape_tail = (SLICES, 2, WIN, OBJ_COLS)
    phase_part = jax.random.uniform(phase_key, shape_tail, jnp.float32, -2.9, 2.9)
    exponent = jax.random.uniform(absorb_key, shape_tail, jnp.float32, -5.29, -3.0)
    absorb = jnp.exp(exponent)
    return jnp.stack([phase_part, absorb]).astype(jnp.float32)


def draw_kernel(key, part):
    angle_key, side_key = jax.random.split(jax.random.fold_in(key, 17))
    theta = jax.random.uniform(angle_key, (), jnp.float32, -3.14159, 3.14159)
    side_angles = jax.random.uniform(side_key, (2 * HALF + 1,), jnp.float32, -3.14159, 3.14159)
    side_size = (0.32 / HALF) ** 0.5
    side_taps = side_size * jnp.stack([jnp.cos(side_angles), jnp.sin(side_angles)])
    centre_mask = (jnp.arange(2 * HALF + 1) == HALF)[None, :]
    centre_vals = 0.6 * jnp.stack([jnp.cos(theta), jnp.sin(theta)])[:, None]
    taps = jnp.where(centre_mask, centre_vals, side_taps)
    return taps.astype(jnp.bfloat16)


def draw_offsets(key, part):
    row_key, col_key, pick_key, inner_key, near_key = jax.random.split(key, 5)
    band_count = WIN // BAND
    probe_ids = jnp.arange(PROBES, dtype=jnp.int32)
    row_bands = jax.random.randint(row_key, (PROBES,), 0, band_count + 1)
    col_start = jax.random.randint(col_key, (PROBES,), 0, COL_SCAN + 1)
    chosen = jax.random.randint(pick_key, (), 0, PROBES)
    partner = (chosen + 1) % PROBES
    if WIN >= COL_SCAN:
        row_bands = jnp.where(probe_ids == chosen, band_count, row_bands)
    else:
        col_start = jnp.where(probe_ids == chosen, COL_SCAN, col_start)
    inner_band = jax.random.randint(inner_key, (), 1, band_count)
    row_bands = jnp.where(probe_ids == partner, inner_band, row_bands)
    chosen_col = jnp.sum(jnp.where(probe_ids == chosen, col_start, 0))
    nearby = jax.random.randint(near_key, (), -(WIN // 2), WIN // 2 + 1)
    partner_col = jnp.clip(chosen_col + nearby, 0, COL_SCAN)
    col_start = jnp.where(probe_ids == partner, partner_col, col_start)
    return jnp.stack([row_bands * BAND, col_start], axis=1).astype(jnp.int32)


def block_levels(own_key, dims, pieces, low, high):
    loudness = 1.0
    for axis_at, blocks in pieces:
        draws = jax.random.uniform(jax.random.fold_in(jax.random.fold_in(own_key, 6), axis_at), (blocks,), jnp.float32, low / len(pieces), high / len(pieces))
        loudness = loudness * jnp.repeat(jnp.exp(draws), dims[axis_at] // blocks).reshape((-1,) + (1,) * (len(dims) - 1 - axis_at))
    return loudness


def centred(key, shape, width, limit, pieces=(), held_as=jnp.bfloat16):
    array = width * jax.random.normal(key, shape, jnp.float32)
    if pieces:
        array = array * block_levels(key, shape, pieces, -0.22, 0.18)
    return jnp.clip(array, -limit, limit).astype(held_as)


def setup_inputs(seed: int = 0) -> dict:
    arg_keys = jax.random.split(jax.random.key(seed), 6)
    return {
        "potential": draw_potential(jax.random.fold_in(arg_keys[5], 71), 0),
        "incident": centred(arg_keys[1], (2, PROBES, WIN, WIN), 1.0, 6.0, ((2, 32),), jnp.float32),
        "measured": jnp.clip(3.0 * jax.random.uniform(arg_keys[2], (PROBES, WIN, WIN), jnp.float32) ** block_levels(arg_keys[2], (PROBES, WIN, WIN), ((1, 32),), -0.2, 0.2), 0.0, 3.0),
        "offsets": draw_offsets(jax.random.fold_in(arg_keys[5], 71), 0),
        "kernel": draw_kernel(jax.random.fold_in(arg_keys[5], 71), 0),
    }


def rounded(field_in):
    return lax.optimization_barrier(field_in.astype(jnp.bfloat16)).astype(jnp.float32)


def complex_conv(field_in, taps_re, taps_im, axis_dim):
    half_width = (taps_re.shape[0] - 1) // 2
    length = field_in.shape[axis_dim]
    widths = [(0, 0), (0, 0), (0, 0)]
    widths[axis_dim] = (half_width, half_width)
    padded = jnp.pad(field_in, widths)
    out_re = jnp.zeros(field_in.shape[1:], jnp.float32)
    out_im = jnp.zeros(field_in.shape[1:], jnp.float32)
    for tap_index in range(2 * half_width + 1):
        shifted = lax.slice_in_dim(padded, tap_index, tap_index + length, axis=axis_dim)
        out_re = out_re + taps_re[tap_index] * shifted[0] - taps_im[tap_index] * shifted[1]
        out_im = out_im + taps_re[tap_index] * shifted[1] + taps_im[tap_index] * shifted[0]
    return jnp.stack([out_re, out_im])


def rotate_rows(field_in, shift_rows, axis_dim):
    doubled = jnp.concatenate([field_in, field_in], axis=axis_dim)
    return lax.dynamic_slice_in_dim(doubled, shift_rows, field_in.shape[axis_dim], axis_dim)


def reference(potential, incident, measured, offsets, kernel):
    taps_re = kernel[0].astype(jnp.float32)
    taps_im = kernel[1].astype(jnp.float32)
    back_re = taps_re[::-1]
    back_im = -taps_im[::-1]
    layered = potential.reshape(2, SLICES, 2 * WIN, OBJ_COLS)
    gradient = jnp.zeros_like(layered)
    for probe_index in range(PROBES):
        row_start = offsets[probe_index, 0].astype(jnp.int32)
        col_start = offsets[probe_index, 1].astype(jnp.int32)
        zero_index = jnp.zeros((), jnp.int32)
        view = lax.dynamic_slice(layered, (zero_index, zero_index, row_start, col_start), (2, SLICES, WIN, WIN))
        damping = jnp.exp(-view[1])
        transmit = jnp.stack([damping * jnp.cos(view[0]), damping * jnp.sin(view[0])])
        shift_rows = (row_start % WIN).astype(jnp.int32)
        wave_now = rounded(rotate_rows(incident[:, probe_index], shift_rows, 1))
        entries = []
        for slice_index in range(SLICES):
            entries.append(wave_now)
            factor = transmit[:, slice_index]
            product = rounded(jnp.stack([factor[0] * wave_now[0] - factor[1] * wave_now[1],
                                         factor[0] * wave_now[1] + factor[1] * wave_now[0]]))
            spread = rounded(complex_conv(product, taps_re, taps_im, 1))
            wave_now = rounded(complex_conv(spread, taps_re, taps_im, 2))
        target = rotate_rows(measured[probe_index], shift_rows, 0)
        residual = wave_now[0] * wave_now[0] + wave_now[1] * wave_now[1] - target
        adjoint = rounded(2.0 * residual[None] * wave_now)
        for slice_index in reversed(range(SLICES)):
            spread = rounded(complex_conv(adjoint, back_re, back_im, 2))
            local_grad = rounded(complex_conv(spread, back_re, back_im, 1))
            factor = transmit[:, slice_index]
            entry_wave = entries[slice_index]
            cross_re = entry_wave[0] * local_grad[0] + entry_wave[1] * local_grad[1]
            cross_im = entry_wave[0] * local_grad[1] - entry_wave[1] * local_grad[0]
            turned_re = factor[0] * cross_re + factor[1] * cross_im
            turned_im = factor[0] * cross_im - factor[1] * cross_re
            corner = (zero_index, zero_index + slice_index, row_start, col_start)
            current = lax.dynamic_slice(gradient, corner, (2, 1, WIN, WIN))
            addition = jnp.stack([turned_im, -turned_re])[:, None]
            gradient = lax.dynamic_update_slice(gradient, current + addition, corner)
            adjoint = rounded(jnp.stack([factor[0] * local_grad[0] + factor[1] * local_grad[1],
                                         factor[0] * local_grad[1] - factor[1] * local_grad[0]]))
    return gradient.reshape(2, SLICES, 2, WIN, OBJ_COLS)
```

```python
import functools

import jax
import jax.numpy as jnp
from jax import lax
from jax.experimental import pallas as pl
from jax.experimental.pallas import tpu as pltpu
from jax.sharding import PartitionSpec as P

F32 = jnp.float32
BF16 = jnp.bfloat16
LANES = 128
VMEM_BYTES = 40 * 1024 * 1024


def vmem_spec():
    return pl.BlockSpec(memory_space=pltpu.VMEM)


def smem_spec():
    return pl.BlockSpec(memory_space=pltpu.SMEM)


def call(body, outs, scalars, arrays, flops, moved):
    return pl.pallas_call(
        body,
        out_shape=outs,
        in_specs=[smem_spec()] * len(scalars) + [vmem_spec()] * len(arrays),
        out_specs=jax.tree.map(lambda _: vmem_spec(), outs),
        compiler_params=pltpu.CompilerParams(vmem_limit_bytes=VMEM_BYTES),
        cost_estimate=pl.CostEstimate(flops=flops, bytes_accessed=moved, transcendentals=0),
    )(*scalars, *arrays)


def prepare_body(dims, meta, potential, incident, measured, sent, start, target):
    probes, tiles, halo, window, columns = dims
    width = 2 * halo + LANES
    span = window + 2 * halo
    lane = lax.broadcasted_iota(jnp.int32, (potential.shape[2], span), 1)
    inside = (lane >= halo) & (lane < window + halo)
    for probe in range(probes):
        half = meta[3 + probe]
        turn = lax.rem(columns + halo - meta[3 + probes + probe], columns)
        phase = pltpu.roll(potential[0, half], turn, 1)[:, :span]
        absorb = pltpu.roll(potential[1, half], turn, 1)[:, :span]
        damping = jnp.where(inside, jnp.exp(-absorb), 0.0)
        real = (damping * jnp.cos(phase)).astype(BF16)
        imag = (damping * jnp.sin(phase)).astype(BF16)
        for tile in range(tiles):
            cols = slice(tile * LANES, tile * LANES + width)
            sent[probe * tiles + tile, 0] = real[:, cols]
            sent[probe * tiles + tile, 1] = imag[:, cols]
    own = meta[0]
    turn = lax.rem(window + halo - meta[1] * LANES, window)
    for part in range(2):
        start[part] = pltpu.roll(incident[part, own], turn, 1)[:, :width].astype(BF16)
    target[...] = pltpu.roll(measured[own], turn, 1)[:, :width]


def banded(taps, base, diff, half_width, conj):
    count = 2 * half_width + 1
    real = jnp.zeros(diff.shape, F32)
    imag = jnp.zeros(diff.shape, F32)
    for tap in range(count):
        hit = diff == tap - half_width
        source = count - 1 - tap if conj else tap
        real = jnp.where(hit, taps[source], real)
        value = taps[count + source]
        imag = jnp.where(hit, -value if conj else value, imag)
    return real, imag


def matrices_body(dims, meta, taps, row_fwd, row_bwd, col_fwd, col_bwd):
    band, window, half_width, width = dims
    rows = 3 * band
    out_row = lax.broadcasted_iota(jnp.int32, (rows, rows), 0)
    in_row = lax.broadcasted_iota(jnp.int32, (rows, rows), 1)
    at = in_row + (meta[2] - 1) * band
    row_diff = jnp.where((at >= 0) & (at < window), in_row - out_row, window)
    in_col = lax.broadcasted_iota(jnp.int32, (width, width), 0)
    out_col = lax.broadcasted_iota(jnp.int32, (width, width), 1)
    for conj, row_out, col_out in ((False, row_fwd, col_fwd), (True, row_bwd, col_bwd)):
        real, imag = banded(taps, meta, row_diff, half_width, conj)
        row_out[:rows] = real.astype(BF16)
        row_out[rows:] = imag.astype(BF16)
        real, imag = banded(taps, meta, in_col - out_col, half_width, conj)
        col_out[:width, :width] = real.astype(BF16)
        col_out[:width, width:] = imag.astype(BF16)
        col_out[width:, :width] = (-imag).astype(BF16)
        col_out[width:, width:] = real.astype(BF16)


def stacked(above, own, below, index):
    return jnp.concatenate([above[index], own[index], below[index]], axis=0).astype(F32)


def spread_rows(matrix, field, width):
    both = jnp.dot(matrix, field, preferred_element_type=F32)
    rows = matrix.shape[1]
    direct, crossed = both[:rows], both[rows:]
    return direct[:, :width] - crossed[:, width:], direct[:, width:] + crossed[:, :width]


def forward_steps(steps, band, width, row_mat, col_mat, above, own, below, psi_re, psi_im, kept):
    for step in range(steps):
        t_re = stacked(above, own, below, (step, 0))
        t_im = stacked(above, own, below, (step, 1))
        product = jnp.concatenate(
            [t_re * psi_re - t_im * psi_im, t_re * psi_im + t_im * psi_re], axis=1
        ).astype(BF16)
        kept[step] = product[band : 2 * band]
        h_re, h_im = spread_rows(row_mat[...], product, width)
        spread = jnp.concatenate([h_re, h_im], axis=1).astype(BF16)
        psi = jnp.dot(spread, col_mat[...], preferred_element_type=F32)
        psi_re, psi_im = psi[:, :width], psi[:, width:]
    return psi_re[band : 2 * band], psi_im[band : 2 * band]


def first_forward_body(dims, row_mat, col_mat, above, own, below, kept, leaving):
    steps, band, width = dims
    psi_re = stacked(above, own, below, (steps, 0))
    psi_im = stacked(above, own, below, (steps, 1))
    psi_re, psi_im = forward_steps(
        steps, band, width, row_mat, col_mat, above, own, below, psi_re, psi_im, kept
    )
    leaving[0] = psi_re.astype(BF16)
    leaving[1] = psi_im.astype(BF16)


def second_forward_body(
    dims, row_mat, col_mat, above, own, below, w_above, w_own, w_below, target, kept, seed
):
    steps, band, width = dims
    psi_re = stacked(w_above, w_own, w_below, 0)
    psi_im = stacked(w_above, w_own, w_below, 1)
    psi_re, psi_im = forward_steps(
        steps, band, width, row_mat, col_mat, above, own, below, psi_re, psi_im, kept
    )
    twice = 2.0 * (psi_re * psi_re + psi_im * psi_im - target[...])
    g_re, g_im = twice * psi_re, twice * psi_im
    low = lax.broadcasted_iota(jnp.int32, (band, LANES), 1) < LANES // 2
    turned = pltpu.roll(g_re[:, :LANES], LANES // 2, 1)
    seed[:, :LANES] = jnp.where(low, turned, g_im[:, :LANES]).astype(BF16)
    turned = pltpu.roll(g_im[:, LANES:], LANES // 2, 1)
    seed[:, LANES:] = jnp.where(low, g_re[:, LANES:], turned).astype(BF16)


def backward_steps(
    steps, first, band, width, row_mat, col_mat, above, own, below, g_re, g_im, kept, terms
):
    field = jnp.concatenate([g_re, g_im], axis=1).astype(BF16)
    for step in reversed(range(steps)):
        spread = jnp.dot(field, col_mat[...], preferred_element_type=F32).astype(BF16)
        w_re, w_im = spread_rows(row_mat[...], spread, width)
        product = kept[step].astype(F32)
        u_re, u_im = product[:, :width], product[:, width:]
        v_re, v_im = w_re[band : 2 * band], w_im[band : 2 * band]
        turned = pltpu.roll(u_re * v_im - u_im * v_re, width - LANES // 2, 1)
        terms[first + step, 0] = turned[:, :LANES].astype(BF16)
        turned = pltpu.roll(-(u_re * v_re + u_im * v_im), width - LANES // 2, 1)
        terms[first + step, 1] = turned[:, :LANES].astype(BF16)
        t_re = stacked(above, own, below, (step, 0))
        t_im = stacked(above, own, below, (step, 1))
        field = jnp.concatenate(
            [t_re * w_re + t_im * w_im, t_re * w_im - t_im * w_re], axis=1
        ).astype(BF16)
    return field


def first_backward_body(
    dims, row_mat, col_mat, above, own, below, seeds, left, right, kept, leaving, terms
):
    steps, band, width = dims
    half = LANES // 2
    middle = seeds[...].reshape(3 * band, 2 * LANES).astype(F32)
    left_in = left[...].reshape(3 * band, LANES).astype(F32)
    right_in = right[...].reshape(3 * band, LANES).astype(F32)
    low = lax.broadcasted_iota(jnp.int32, (3 * band, LANES), 1) < half
    first, last = middle[:, :LANES], middle[:, LANES:]
    g_re = jnp.concatenate(
        [
            jnp.where(low, left_in, pltpu.roll(first, half, 1)),
            jnp.where(low, last, pltpu.roll(right_in, half, 1)),
        ],
        axis=1,
    )
    g_im = jnp.concatenate(
        [
            jnp.where(low, pltpu.roll(left_in, half, 1), first),
            jnp.where(low, pltpu.roll(last, half, 1), right_in),
        ],
        axis=1,
    )
    field = backward_steps(
        steps, 0, band, width, row_mat, col_mat, above, own, below, g_re, g_im, kept, terms
    )
    leaving[0] = field[band : 2 * band, :width]
    leaving[1] = field[band : 2 * band, width:]


def second_backward_body(
    dims, row_mat, col_mat, above, own, below, w_above, w_own, w_below, kept, later, terms
):
    steps, band, width = dims
    terms[steps:] = later[...]
    g_re = stacked(w_above, w_own, w_below, 0)
    g_im = stacked(w_above, w_own, w_below, 1)
    backward_steps(
        steps, 0, band, width, row_mat, col_mat, above, own, below, g_re, g_im, kept, terms
    )


def collect_body(dims, meta, terms, gradient):
    probes, tiles, window, columns = dims
    band = terms.shape[2]
    rest = jnp.zeros((band, columns - window), F32)
    for part in range(2):
        moved = []
        for probe in range(probes):
            pieces = [terms[probe * tiles + tile, part].astype(F32) for tile in range(tiles)]
            row = jnp.concatenate(pieces + [rest], axis=1)
            moved.append(pltpu.roll(row, meta[3 + probes + probe], 1))
        for half in range(2):
            total = jnp.zeros((band, columns), F32)
            for probe in range(probes):
                total = total + jnp.where(meta[3 + probe] == half, moved[probe], 0.0)
            gradient[part, half] = total


def local(potential, incident, measured, offsets, kernel):
    lat_count = lax.axis_size("lat")
    depth_count = lax.axis_size("depth")
    lat_index = lax.axis_index("lat")
    depth_index = lax.axis_index("depth")
    band = potential.shape[3]
    columns = potential.shape[4]
    window = incident.shape[3]
    probes = incident.shape[1]
    half_width = (kernel.shape[1] - 1) // 2
    tiles = depth_count // probes
    steps = depth_count // 2
    halo = depth_count * half_width
    width = 2 * halo + LANES

    first_band = offsets[:, 0] // band
    place = (lat_index - first_band) % lat_count
    halves = (first_band + place) // lat_count
    own_probe = depth_index // tiles
    head = jnp.stack([own_probe, depth_index % tiles, jnp.where(own_probe == 0, place[0], place[1])])
    meta = jnp.concatenate([head, halves, offsets[:, 1]]).astype(jnp.int32)
    taps = kernel.astype(F32).reshape(-1)

    downward = [(i, (i + 1) % lat_count) for i in range(lat_count)]
    upward = [((i + 1) % lat_count, i) for i in range(lat_count)]
    inner = [i for i in range(depth_count - 1) if (i + 1) % tiles]

    def row_halo(cells):
        return lax.ppermute(cells, "lat", downward), lax.ppermute(cells, "lat", upward)

    def shape(*dims, dtype=BF16):
        return jax.ShapeDtypeStruct(dims, dtype)

    rows = 3 * band
    sent, start, target = call(
        functools.partial(prepare_body, (probes, tiles, halo, window, columns)),
        (
            shape(depth_count, 2, band, width),
            shape(2, band, width),
            shape(band, width, dtype=F32),
        ),
        [meta],
        [potential[:, 0], incident, measured],
        10_000_000,
        3_000_000,
    )
    row_fwd, row_bwd, col_fwd, col_bwd = call(
        functools.partial(matrices_body, (band, window, half_width, width)),
        (
            shape(2 * rows, rows),
            shape(2 * rows, rows),
            shape(2 * width, 2 * width),
            shape(2 * width, 2 * width),
        ),
        [meta, taps],
        [],
        10_000_000,
        1_500_000,
    )
    layers = lax.all_to_all(sent, "depth", 0, 0, tiled=False)
    early = jnp.concatenate([layers[:steps], start[None]], axis=0)
    early_above, early_below = row_halo(early)
    late = layers[steps:]
    late, early_above, early_below = lax.optimization_barrier((late, early_above, early_below))
    late_above, late_below = row_halo(late)

    flops = 2 * steps * rows * 2 * width * (2 * rows + 2 * width)
    moved = 6 * steps * rows * width
    sizes = (steps, band, width)
    kept_early, wave = call(
        functools.partial(first_forward_body, sizes),
        (shape(steps, band, 2 * width), shape(2, band, width)),
        [],
        [row_fwd, col_fwd, early_above, early, early_below],
        flops,
        moved,
    )
    wave_above, wave_below = row_halo(wave)
    kept_late, seed = call(
        functools.partial(second_forward_body, sizes),
        (shape(steps, band, 2 * width), shape(band, 2 * LANES)),
        [],
        [row_fwd, col_fwd, late_above, late, late_below, wave_above, wave, wave_below, target],
        flops,
        moved,
    )
    seed_above, seed_below = row_halo(seed)
    seeds = jnp.stack([seed_above, seed, seed_below])
    from_left = lax.ppermute(seeds[:, :, LANES:], "depth", [(i, i + 1) for i in inner])
    from_right = lax.ppermute(seeds[:, :, :LANES], "depth", [(i + 1, i) for i in inner])
    adjoint, terms_late = call(
        functools.partial(first_backward_body, sizes),
        (shape(2, band, width), shape(steps, 2, band, LANES)),
        [],
        [
            row_bwd,
            col_bwd,
            late_above,
            late,
            late_below,
            seeds,
            from_left,
            from_right,
            kept_late,
        ],
        flops,
        moved,
    )
    adjoint_above, adjoint_below = row_halo(adjoint)
    terms = call(
        functools.partial(second_backward_body, sizes),
        shape(2 * steps, 2, band, LANES),
        [],
        [
            row_bwd,
            col_bwd,
            early_above,
            early,
            early_below,
            adjoint_above,
            adjoint,
            adjoint_below,
            kept_early,
            terms_late,
        ],
        flops,
        moved,
    )
    gathered = lax.all_to_all(terms, "depth", 0, 0, tiled=False)
    gradient = call(
        functools.partial(collect_body, (probes, tiles, window, columns)),
        shape(2, 2, band, columns, dtype=F32),
        [meta],
        [gathered],
        1_000_000,
        2_000_000,
    )
    return gradient[:, None]


def solution(mesh):
    in_specs = (
        P(None, "depth", None, "lat", None),
        P(None, None, "lat", None),
        P(None, "lat", None),
        P(),
        P(),
    )
    out_specs = P(None, "depth", None, "lat", None)
    return jax.shard_map(local, mesh=mesh, in_specs=in_specs, out_specs=out_specs, check_vma=False)
```

```python
import functools

import jax
import jax.numpy as jnp
from jax import lax
from jax.experimental import pallas as pl
from jax.experimental.pallas import tpu as pltpu
from jax.sharding import Mesh
from jax.sharding import PartitionSpec as P

F32 = jnp.float32
BF16 = jnp.bfloat16
LANES = 128
PIECE = 64
CORES = 2
GROUP = 4
TAIL = 8
VMEM_BYTES = 48 * 1024 * 1024


def vmem_spec():
    return pl.BlockSpec(memory_space=pltpu.VMEM)


def smem_spec():
    return pl.BlockSpec(memory_space=pltpu.SMEM)


def call(body, outs, scalars, arrays, cost, scratch=(), outside=0):
    in_specs = [smem_spec()] * len(scalars)
    in_specs += [pl.BlockSpec(memory_space=pl.ANY)] * outside
    in_specs += [vmem_spec()] * (len(arrays) - outside)
    return pl.pallas_call(
        body,
        out_shape=outs,
        in_specs=in_specs,
        out_specs=jax.tree.map(lambda _: vmem_spec(), outs),
        scratch_shapes=list(scratch),
        compiler_params=pltpu.CompilerParams(vmem_limit_bytes=VMEM_BYTES),
        cost_estimate=pl.CostEstimate(flops=cost[0], bytes_accessed=cost[1], transcendentals=0),
    )(*scalars, *arrays)


def tile_at(x, y, y_count, probes):
    rows = y_count // probes
    probe, row = y // rows, y % rows
    return probe, row * GROUP + (x if row % 2 == 0 else GROUP - 1 - x)


def low_lanes(rows):
    return lax.broadcasted_iota(jnp.int32, (rows, LANES), 1) < PIECE


def swap_halves(cells):
    return pltpu.roll(cells, PIECE, 1)


def half_of(offsets, probe, band, lat, lat_count):
    first = offsets[probe, 0] // band
    return (first + lax.rem(lat - first + lat_count, lat_count)) // lat_count


def packed(real, imag, tiles):
    span = real.shape[1]
    real_on = pltpu.roll(real, span - PIECE, 1)
    imag_on = pltpu.roll(imag, span - PIECE, 1)
    low = low_lanes(real.shape[0])
    out = []
    for tile in range(tiles):
        base = tile // 2 * LANES
        here, there = slice(base, base + LANES), slice(base + LANES, base + 2 * LANES)
        if tile % 2 == 0:
            middle = jnp.where(low, real[:, there], imag_on[:, here])
            out.append((real[:, here], middle, imag[:, here]))
        else:
            middle = jnp.where(low, real_on[:, there], imag[:, there])
            out.append((real_on[:, here], middle, imag_on[:, here]))
    return out


def prepare_body(
    dims, offsets, potential, incident, measured, sent, pot_buf, inc_buf, mea_buf, sems
):
    probes, tiles, halo, y_count, lat_count = dims
    band, columns = pot_buf.shape[2], pot_buf.shape[3]
    window = inc_buf.shape[3]
    span = window + 2 * halo
    y = lax.axis_index("y")
    lat = lax.axis_index("z") * GROUP + lax.axis_index("x")
    strip = TAIL // 2
    first = pl.multiple_of(y // 2 * TAIL, TAIL)
    copies = []
    for probe in range(probes):
        half = half_of(offsets, probe, band, lat, lat_count)
        copies.append(
            pltpu.make_async_copy(potential.at[:, half], pot_buf.at[probe], sems.at[probe])
        )
    copies.append(
        pltpu.make_async_copy(incident.at[:, :, pl.ds(first, TAIL)], inc_buf, sems.at[probes])
    )
    copies.append(
        pltpu.make_async_copy(measured.at[:, pl.ds(first, TAIL)], mea_buf, sems.at[probes + 1])
    )
    for copy in copies:
        copy.start()
    slots = {}
    for spot in range(y_count * GROUP):
        slots[tile_at(spot // y_count, spot % y_count, y_count, probes)] = spot
    lane = lax.broadcasted_iota(jnp.int32, (band, span), 1)
    inside = (lane >= halo) & (lane < window + halo)
    for probe in range(probes):
        copies[probe].wait()
        turn = lax.rem(columns + halo - offsets[probe, 1], columns)
        phase = pltpu.roll(pot_buf[probe, 0], turn, 1)[:, :span]
        absorb = pltpu.roll(pot_buf[probe, 1], turn, 1)[:, :span]
        damping = jnp.where(inside, jnp.exp(-absorb), 0.0)
        for tile, parts in enumerate(
            packed(damping * jnp.cos(phase), damping * jnp.sin(phase), tiles)
        ):
            for at, part in enumerate(parts):
                cols = slice(at * LANES, (at + 1) * LANES)
                sent[slots[probe, tile], :band, cols] = part.astype(BF16)
    copies[probes].wait()
    copies[probes + 1].wait()
    odd = lax.rem(y, 2) == 1
    rest = jnp.zeros((TAIL, 2 * halo), F32)
    upper = lax.broadcasted_iota(jnp.int32, (TAIL, LANES), 0) < strip
    low = low_lanes(TAIL)
    for probe in range(probes):
        wide = []
        for part in range(2):
            rows = inc_buf[part, probe]
            rows = jnp.where(odd, pltpu.roll(rows, strip, 0), rows)
            wide.append(pltpu.roll(jnp.concatenate([rows, rest], axis=1), halo, 1))
        rows = mea_buf[probe]
        rows = jnp.where(odd, rows, pltpu.roll(rows, strip, 0))
        coarse = rows.astype(BF16).astype(F32)
        fine = rows - coarse
        coarse_on = pltpu.roll(coarse, window - PIECE, 1)
        fine_back = pltpu.roll(fine, PIECE, 1)
        for tile, parts in enumerate(packed(wide[0], wide[1], tiles)):
            here = slice(tile // 2 * LANES, tile // 2 * LANES + LANES)
            if tile % 2 == 0:
                both = jnp.where(low, coarse[:, here], fine_back[:, here])
            else:
                both = jnp.where(low, coarse_on[:, here], fine[:, here])
            for at, part in enumerate(parts):
                cols = slice(at * LANES, (at + 1) * LANES)
                under = both if at == 0 else jnp.zeros_like(both)
                sent[slots[probe, tile], band:, cols] = jnp.where(upper, part, under).astype(BF16)


def banded(taps, diff, half_width, conj):
    count = 2 * half_width + 1
    real = jnp.zeros(diff.shape, F32)
    imag = jnp.zeros(diff.shape, F32)
    for tap in range(count):
        hit = diff == tap - half_width
        source = count - 1 - tap if conj else tap
        real = jnp.where(hit, taps[source], real)
        value = taps[count + source]
        imag = jnp.where(hit, -value if conj else value, imag)
    return real, imag


def matrices_body(dims, offsets, taps, row_fwd, row_bwd, col_fwd, col_bwd):
    band, half_width, y_count, probes, lat_count = dims
    rows, lanes = row_fwd.shape[0], col_fwd.shape[0]
    reach = rows // band // 2 - GROUP // 2
    own = lax.axis_index("y") // (y_count // probes)
    base = lax.axis_index("z") * GROUP - reach - offsets[own, 0] // band + 2 * lat_count
    base = lax.rem(base, lat_count)

    def window_row(axis):
        index = lax.broadcasted_iota(jnp.int32, (rows, rows), axis)
        return jnp.where(
            index // band + base >= lat_count, index + (base - lat_count) * band, index + base * band
        )

    def column(axis):
        index = lax.broadcasted_iota(jnp.int32, (lanes, lanes), axis)
        edge = LANES + PIECE
        other = index >= edge
        return jnp.where(index >= 2 * LANES, index - 2 * LANES, jnp.where(other, index - PIECE, index)), other

    row_diff = window_row(1) - window_row(0)
    in_col, in_imag = column(0)
    out_col, out_imag = column(1)
    for conj, row_out, col_out in ((False, row_fwd, col_fwd), (True, row_bwd, col_bwd)):
        real, imag = banded(taps, row_diff, half_width, conj)
        row_out[:, :rows] = real.astype(BF16)
        row_out[:, rows:] = imag.astype(BF16)
        real, imag = banded(taps, in_col - out_col, half_width, conj)
        signed = jnp.where(in_imag, -imag, imag)
        col_out[...] = jnp.where(in_imag == out_imag, real, signed).astype(BF16)


def three(cells):
    return cells[:, :LANES], cells[:, LANES : 2 * LANES], cells[:, 2 * LANES :]


def fill_layer(layer, source, y, band):
    at = 0
    for part in source:
        for index in range(part.shape[0]):
            layer[at : at + band] = part[index, y, :band]
            at += band


def turning(middle, low):
    turned = swap_halves(middle)
    return jnp.where(low, middle, turned), jnp.where(low, -turned, middle)


def with_quarter_turn(parts, low):
    first, middle, last = parts
    turned = swap_halves(middle)
    direct = jnp.concatenate([first, middle, last], axis=1)
    crossed = jnp.concatenate([-last, jnp.where(low, -turned, turned), first], axis=1)
    return jnp.concatenate([direct, crossed], axis=0).astype(BF16)


def forward_body(
    dims, row_mat, col_mat, above, own, below, o_above, o_own, o_below, kept, seed, psi, layer, goal
):
    band, strip = dims
    near, far = (above, own, below), (o_above, o_own, o_below)
    core = lax.axis_index("core")
    rows = psi.shape[0]
    own_rows = own.shape[0] * band
    head = (rows - own_rows) // 2
    y_count = own.shape[1]
    low = low_lanes(rows)
    upper = lax.broadcasted_iota(jnp.int32, (TAIL, 3 * LANES), 0) < strip
    at = 0
    for part in near:
        for index in range(part.shape[0]):
            for pair in range(y_count // 2):
                one = part[index, 2 * pair, band:].astype(F32)
                two = part[index, 2 * pair + 1, band:].astype(F32)
                psi[at : at + TAIL] = jnp.where(upper, one, pltpu.roll(two, strip, 0))
                if part is own:
                    both = jnp.where(upper, pltpu.roll(one, strip, 0), two)[:, :LANES]
                    goal[at - head : at - head + TAIL] = both + swap_halves(both)
                at += TAIL

    def two_slices(y, _):
        for parity in range(CORES):
            mine = core == parity
            pl.when(mine)(lambda: fill_layer(layer, near, y, band))
            pl.when(jnp.logical_not(mine))(lambda: fill_layer(layer, far, y, band))
            t_first, t_middle, t_last = three(layer[...].astype(F32))
            t_real, t_turn = turning(t_middle, low)
            first, middle, last = three(psi[...])
            u_first = t_first * first - t_last * last
            u_last = t_first * last + t_last * first
            u_middle = t_real * middle + t_turn * swap_halves(middle)
            kept[CORES * y + parity, :, :LANES] = u_first[head : head + own_rows].astype(BF16)
            kept[CORES * y + parity, :, LANES:] = u_last[head : head + own_rows].astype(BF16)
            field = with_quarter_turn((u_first, u_middle, u_last), low)
            spread = jnp.dot(row_mat[...], field, preferred_element_type=F32).astype(BF16)
            psi[...] = jnp.dot(spread, col_mat[...], preferred_element_type=F32)
        return 0

    lax.fori_loop(0, y_count, two_slices, 0)
    real = psi[head : head + own_rows, :LANES]
    imag = psi[head : head + own_rows, 2 * LANES :]
    low = low_lanes(own_rows)
    twice = 2.0 * (real * real + imag * imag - goal[...])
    seed[...] = jnp.where(low, swap_halves(twice * real), twice * imag).astype(BF16)


def backward_body(
    dims,
    row_mat,
    col_mat,
    above,
    own,
    below,
    o_above,
    o_own,
    o_below,
    kept,
    seeds,
    left,
    right,
    terms,
    field,
    layer,
):
    (band,) = dims
    near, far = (above, own, below), (o_above, o_own, o_below)
    core = lax.axis_index("core")
    rows = field.shape[0]
    own_rows = own.shape[0] * band
    head = (rows - own_rows) // 2
    y_count = own.shape[1]
    low = low_lanes(rows)
    low_own = low_lanes(own_rows)
    middle = seeds[...].astype(F32)
    beside = left[...].astype(F32)
    field[:, :LANES] = jnp.where(low, beside, swap_halves(middle)).astype(BF16)
    field[:, LANES : 2 * LANES] = right[...]
    field[:, 2 * LANES :] = jnp.where(low, swap_halves(beside), middle).astype(BF16)

    def two_slices(step, _):
        y = y_count - 1 - step
        for parity in reversed(range(CORES)):
            mine = core == parity
            pl.when(mine)(lambda: fill_layer(layer, near, y, band))
            pl.when(jnp.logical_not(mine))(lambda: fill_layer(layer, far, y, band))
            spread = jnp.dot(field[...], col_mat[...], preferred_element_type=F32)
            both = with_quarter_turn(three(spread), low)
            first, centre, last = three(
                jnp.dot(row_mat[...], both, preferred_element_type=F32)
            )

            @pl.when(mine)
            def _():
                u_re = kept[CORES * y + parity, :, :LANES].astype(F32)
                u_im = kept[CORES * y + parity, :, LANES:].astype(F32)
                v_re, v_im = first[head : head + own_rows], last[head : head + own_rows]
                phase = swap_halves(u_re * v_im - u_im * v_re)
                term = jnp.where(low_own, phase, -(u_re * v_re + u_im * v_im)).astype(BF16)
                for index in range(own.shape[0]):
                    terms[index, y] = term[index * band : (index + 1) * band]

            t_first, t_middle, t_last = three(layer[...].astype(F32))
            t_real, t_turn = turning(t_middle, low)
            field[:, :LANES] = (t_first * first + t_last * last).astype(BF16)
            turned = t_real * centre - t_turn * swap_halves(centre)
            field[:, LANES : 2 * LANES] = turned.astype(BF16)
            field[:, 2 * LANES :] = (t_first * last - t_last * first).astype(BF16)
        return 0

    lax.fori_loop(0, y_count, two_slices, 0)


def collect_body(dims, offsets, terms, gradient):
    probes, tiles, y_count, lat_count, window, columns = dims
    band = terms.shape[1]
    lat = lax.axis_index("z") * GROUP + lax.axis_index("x")
    slots = {}
    for spot in range(y_count * GROUP):
        slots[tile_at(spot // y_count, spot % y_count, y_count, probes)] = spot
    low = low_lanes(band)
    rest = jnp.zeros((band, columns - window), F32)
    moved = []
    for probe in range(probes):
        parts = ([], [])
        for pair in range(tiles // 2):
            one = terms[slots[probe, 2 * pair]].astype(F32)
            two = terms[slots[probe, 2 * pair + 1]].astype(F32)
            parts[0].append(jnp.where(low, one, swap_halves(two)))
            parts[1].append(jnp.where(low, swap_halves(one), two))
        half = half_of(offsets, probe, band, lat, lat_count)
        for part in range(2):
            row = pltpu.roll(jnp.concatenate(parts[part] + [rest], axis=1), offsets[probe, 1], 1)
            moved.append((part, half, row))
    for part in range(2):
        for at in range(2):
            total = jnp.zeros((band, columns), F32)
            for which, half, row in moved:
                if which == part:
                    total = total + jnp.where(half == at, row, 0.0)
            gradient[part, at] = total


def local(potential, incident, measured, offsets, kernel):
    y_count = lax.axis_size("y")
    z_count = lax.axis_size("z")
    lat_count = z_count * GROUP
    band = potential.shape[3]
    columns = potential.shape[4]
    window = incident.shape[3]
    probes = incident.shape[1]
    half_width = (kernel.shape[1] - 1) // 2
    slices = y_count * CORES
    halo = slices * half_width
    tiles = y_count * GROUP // probes
    spots = y_count * GROUP
    reach = halo // band
    rows = (GROUP + 2 * reach) * band
    own_rows = GROUP * band
    lanes = 3 * LANES
    taps = kernel.astype(F32).reshape(-1)

    def shape(*dims, dtype=BF16):
        return jax.ShapeDtypeStruct(dims, dtype)

    sent = call(
        functools.partial(prepare_body, (probes, tiles, halo, y_count, lat_count)),
        shape(spots, band + TAIL, lanes),
        [offsets],
        [potential[:, 0], incident, measured],
        (20_000_000, 3_000_000),
        [
            pltpu.VMEM((probes, 2, band, columns), F32),
            pltpu.VMEM((2, probes, TAIL, window), F32),
            pltpu.VMEM((probes, TAIL, window), F32),
            pltpu.SemaphoreType.DMA((probes + 2,)),
        ],
        outside=3,
    )
    row_fwd, row_bwd, col_fwd, col_bwd = call(
        functools.partial(matrices_body, (band, half_width, y_count, probes, lat_count)),
        (
            shape(rows, 2 * rows),
            shape(rows, 2 * rows),
            shape(lanes, lanes),
            shape(lanes, lanes),
        ),
        [offsets, taps],
        [],
        (20_000_000, 1_500_000),
    )

    down_z = [(i, (i + 1) % z_count) for i in range(z_count)]
    up_z = [((i + 1) % z_count, i) for i in range(z_count)]

    def row_halo(last, first):
        return lax.ppermute(last, "z", down_z), lax.ppermute(first, "z", up_z)

    def other_core(cells):
        return lax.ppermute(cells, "core", [(i, CORES - 1 - i) for i in range(CORES)])

    own = lax.all_to_all(sent, ("x", "y"), 0, 0, tiled=False)
    own = own.reshape(GROUP, y_count, band + TAIL, lanes)
    above, below = row_halo(own[GROUP - reach :], own[:reach])
    layers = (above, own, below)
    layers = layers + tuple(other_core(part) for part in layers)

    flops = 2 * slices * rows * lanes * (2 * rows + lanes)
    kept, seed = call(
        functools.partial(forward_body, (band, TAIL // 2)),
        (shape(slices, own_rows, 2 * LANES), shape(own_rows, LANES)),
        [],
        [row_fwd, col_fwd, *layers],
        (flops, 6_000_000),
        [
            pltpu.VMEM((rows, lanes), F32),
            pltpu.VMEM((rows, lanes), BF16),
            pltpu.VMEM((own_rows, LANES), F32),
        ],
    )
    seed_above, seed_below = row_halo(seed[own_rows - halo :], seed[:halo])
    seeds = jnp.concatenate([seed_above, seed, seed_below], axis=0)
    at = {}
    for y in range(y_count):
        for x in range(GROUP):
            at[tile_at(x, y, y_count, probes)] = y * GROUP + x
    right = [(at[p, c], at[p, c + 1]) for p in range(probes) for c in range(tiles - 1)]
    from_left = lax.ppermute(seeds, ("y", "x"), right)
    from_right = lax.ppermute(seeds, ("y", "x"), [(b, a) for a, b in right])
    terms = call(
        functools.partial(backward_body, (band,)),
        shape(GROUP, y_count, band, LANES),
        [],
        [row_bwd, col_bwd, *layers, kept, seeds, from_left, from_right],
        (flops, 6_000_000),
        [pltpu.VMEM((rows, lanes), BF16), pltpu.VMEM((rows, lanes), BF16)],
    )
    gathered = lax.all_to_all(
        terms.reshape(spots, band, LANES), ("x", "y"), 0, 0, tiled=False
    )
    gradient = call(
        functools.partial(collect_body, (probes, tiles, y_count, lat_count, window, columns)),
        shape(2, 2, band, columns, dtype=F32),
        [offsets],
        [gathered],
        (1_000_000, 2_000_000),
    )
    return gradient[:, None]


def solution(mesh):
    depth_count, lat_count = mesh.devices.shape
    grid = mesh.devices.reshape(depth_count // CORES, CORES, lat_count // GROUP, GROUP)
    fine = Mesh(grid, ("y", "core", "z", "x"))
    depth, lat = ("y", "core"), ("z", "x")
    in_specs = (
        P(None, depth, None, lat, None),
        P(None, None, lat, None),
        P(None, lat, None),
        P(),
        P(),
    )
    out_specs = P(None, depth, None, lat, None)
    return jax.shard_map(local, mesh=fine, in_specs=in_specs, out_specs=out_specs, check_vma=False)
```

```python
import functools

import jax
import jax.numpy as jnp
from jax import lax
from jax.experimental import pallas as pl
from jax.experimental.pallas import tpu as pltpu
from jax.sharding import Mesh
from jax.sharding import PartitionSpec as P

F32 = jnp.float32
BF16 = jnp.bfloat16
LANES = 128
PIECE = 64
CORES = 2
GROUP = 4
TAIL = 8
VMEM_BYTES = 16 * 1024 * 1024
WIDE_BYTES = 60 * 1024 * 1024


def vmem_spec():
    return pl.BlockSpec(memory_space=pltpu.VMEM)


def smem_spec():
    return pl.BlockSpec(memory_space=pltpu.SMEM)


def call(body, outs, scalars, arrays, cost, scratch=(), outside=0, grant=VMEM_BYTES):
    in_specs = [smem_spec()] * len(scalars)
    in_specs += [pl.BlockSpec(memory_space=pltpu.HBM)] * outside
    in_specs += [vmem_spec()] * (len(arrays) - outside)
    return pl.pallas_call(
        body,
        out_shape=outs,
        in_specs=in_specs,
        out_specs=jax.tree.map(lambda _: vmem_spec(), outs),
        scratch_shapes=list(scratch),
        compiler_params=pltpu.CompilerParams(vmem_limit_bytes=grant),
        cost_estimate=pl.CostEstimate(flops=cost[0], bytes_accessed=cost[1], transcendentals=0),
    )(*scalars, *arrays)


def tile_at(x, y, y_count, probes):
    rows = y_count // probes
    probe, row = y // rows, y % rows
    return probe, row * GROUP + (x if row % 2 == 0 else GROUP - 1 - x)


def low_lanes(rows):
    return lax.broadcasted_iota(jnp.int32, (rows, LANES), 1) < PIECE


def swap_halves(cells):
    return pltpu.roll(cells, PIECE, 1)


def half_of(offsets, probe, band, lat, lat_count):
    first = offsets[probe, 0] // band
    return (first + lax.rem(lat - first + lat_count, lat_count)) // lat_count


def packed(real, imag, tiles):
    span = real.shape[1]
    real_on = pltpu.roll(real, span - PIECE, 1)
    imag_on = pltpu.roll(imag, span - PIECE, 1)
    low = low_lanes(real.shape[0])
    out = []
    for tile in range(tiles):
        base = tile // 2 * LANES
        here, there = slice(base, base + LANES), slice(base + LANES, base + 2 * LANES)
        if tile % 2 == 0:
            middle = jnp.where(low, real[:, there], imag_on[:, here])
            out.append((real[:, here], middle, imag[:, here]))
        else:
            middle = jnp.where(low, real_on[:, there], imag[:, there])
            out.append((real_on[:, here], middle, imag_on[:, here]))
    return out


def prepare_body(
    dims, offsets, potential, incident, measured, sent, pot_buf, inc_buf, mea_buf, sems
):
    probes, tiles, halo, y_count, lat_count = dims
    band, columns = pot_buf.shape[2], pot_buf.shape[3]
    window = inc_buf.shape[3]
    span = window + 2 * halo
    y = lax.axis_index("y")
    lat = lax.axis_index("z") * GROUP + lax.axis_index("x")
    strip = TAIL // 2
    first = pl.multiple_of(y // 2 * TAIL, TAIL)
    copies = []
    for probe in range(probes):
        half = half_of(offsets, probe, band, lat, lat_count)
        copies.append(
            pltpu.make_async_copy(potential.at[:, half], pot_buf.at[probe], sems.at[probe])
        )
    copies.append(
        pltpu.make_async_copy(incident.at[:, :, pl.ds(first, TAIL)], inc_buf, sems.at[probes])
    )
    copies.append(
        pltpu.make_async_copy(measured.at[:, pl.ds(first, TAIL)], mea_buf, sems.at[probes + 1])
    )
    for copy in copies:
        copy.start()
    slots = {}
    for spot in range(y_count * GROUP):
        slots[tile_at(spot // y_count, spot % y_count, y_count, probes)] = spot
    lane = lax.broadcasted_iota(jnp.int32, (band, span), 1)
    inside = (lane >= halo) & (lane < window + halo)
    for probe in range(probes):
        copies[probe].wait()
        turn = lax.rem(columns + halo - offsets[probe, 1], columns)
        phase = pltpu.roll(pot_buf[probe, 0], turn, 1)[:, :span]
        absorb = pltpu.roll(pot_buf[probe, 1], turn, 1)[:, :span]
        damping = jnp.where(inside, jnp.exp(-absorb), 0.0)
        for tile, parts in enumerate(
            packed(damping * jnp.cos(phase), damping * jnp.sin(phase), tiles)
        ):
            for at, part in enumerate(parts):
                cols = slice(at * LANES, (at + 1) * LANES)
                sent[slots[probe, tile], :band, cols] = part.astype(BF16)
    copies[probes].wait()
    copies[probes + 1].wait()
    odd = lax.rem(y, 2) == 1
    rest = jnp.zeros((TAIL, 2 * halo), F32)
    upper = lax.broadcasted_iota(jnp.int32, (TAIL, LANES), 0) < strip
    low = low_lanes(TAIL)
    for probe in range(probes):
        wide = []
        for part in range(2):
            rows = inc_buf[part, probe]
            rows = jnp.where(odd, pltpu.roll(rows, strip, 0), rows)
            wide.append(pltpu.roll(jnp.concatenate([rows, rest], axis=1), halo, 1))
        rows = mea_buf[probe]
        rows = jnp.where(odd, rows, pltpu.roll(rows, strip, 0))
        coarse = rows.astype(BF16).astype(F32)
        fine = rows - coarse
        coarse_on = pltpu.roll(coarse, window - PIECE, 1)
        fine_back = pltpu.roll(fine, PIECE, 1)
        for tile, parts in enumerate(packed(wide[0], wide[1], tiles)):
            here = slice(tile // 2 * LANES, tile // 2 * LANES + LANES)
            if tile % 2 == 0:
                both = jnp.where(low, coarse[:, here], fine_back[:, here])
            else:
                both = jnp.where(low, coarse_on[:, here], fine[:, here])
            for at, part in enumerate(parts):
                cols = slice(at * LANES, (at + 1) * LANES)
                under = both if at == 0 else jnp.zeros_like(both)
                sent[slots[probe, tile], band:, cols] = jnp.where(upper, part, under).astype(BF16)


def banded(taps, diff, half_width, conj):
    count = 2 * half_width + 1
    real = jnp.zeros(diff.shape, F32)
    imag = jnp.zeros(diff.shape, F32)
    for tap in range(count):
        hit = diff == tap - half_width
        source = count - 1 - tap if conj else tap
        real = jnp.where(hit, taps[source], real)
        value = taps[count + source]
        imag = jnp.where(hit, -value if conj else value, imag)
    return real, imag


def matrices_body(dims, offsets, taps, *outs):
    band, half_width, y_count, probes, lat_count, reach, phase_rows = dims
    own = lax.axis_index("y") // (y_count // probes)
    start = lax.axis_index("z") * GROUP + lax.axis_index("core") * (GROUP // CORES) - reach
    base = lax.rem(start - offsets[own, 0] // band + 2 * lat_count, lat_count)

    def window_row(rows, axis):
        skip = (phase_rows[0] - rows) // 2
        index = lax.broadcasted_iota(jnp.int32, (rows, rows), axis) + skip
        at = index + base * band
        return jnp.where(at >= lat_count * band, at - lat_count * band, at)

    def column(lanes, axis):
        index = lax.broadcasted_iota(jnp.int32, (lanes, lanes), axis)
        if lanes == 2 * LANES:
            return jnp.where(index >= LANES, index - LANES, index), index >= LANES
        imag = index >= LANES + PIECE
        inner = jnp.where(imag, index - PIECE, index)
        return jnp.where(index >= 2 * LANES, index - 2 * LANES, inner), imag

    count = len(phase_rows)
    for at, rows in enumerate(phase_rows):
        diff = window_row(rows, 1) - window_row(rows, 0)
        for conj in (False, True):
            real, imag = banded(taps, diff, half_width, conj)
            out = outs[at + count * conj]
            out[...] = jnp.concatenate([real, imag], axis=1).astype(BF16)
    for at in range(2):
        lanes = outs[2 * count + at].shape[0]
        in_col, in_imag = column(lanes, 0)
        out_col, out_imag = column(lanes, 1)
        for conj in (False, True):
            real, imag = banded(taps, in_col - out_col, half_width, conj)
            signed = jnp.where(in_imag, -imag, imag)
            outs[2 * count + at + 2 * conj][...] = jnp.where(
                in_imag == out_imag, real, signed
            ).astype(BF16)


def parts_of(cells):
    return tuple(cells[:, at : at + LANES] for at in range(0, cells.shape[1], LANES))


def fill_layer(layer, own, halo, y, band, core):
    reach = halo.shape[0] * band
    for index in range(own.shape[0]):
        layer[reach + index * band : reach + (index + 1) * band] = own[index, y, :band]
    base = core * (reach + own.shape[0] * band)
    for index in range(halo.shape[0]):
        at = pl.multiple_of(base + index * band, band)
        layer[pl.ds(at, band)] = halo[index, y, :band]


def narrowed(wide):
    first, middle, last = wide
    edge = lax.broadcasted_iota(jnp.int32, first.shape, 1) < LANES - PIECE // 2
    on, back = LANES - PIECE // 2, PIECE // 2
    real = jnp.where(edge, pltpu.roll(first, on, 1), pltpu.roll(middle, on, 1))
    imag = jnp.where(edge, pltpu.roll(last, on, 1), pltpu.roll(middle, back, 1))
    return real, imag


def own_columns(parts, rows):
    low = low_lanes(rows)
    if len(parts) == 3:
        return jnp.where(low, swap_halves(parts[0]), parts[2])
    real = pltpu.roll(parts[0], LANES - PIECE // 2, 1)
    return jnp.where(low, real, pltpu.roll(parts[1], PIECE // 2, 1))


def times(t, field, conj):
    sign = -1.0 if conj else 1.0
    if len(t) == 2:
        return (
            t[0] * field[0] - sign * (t[1] * field[1]),
            t[0] * field[1] + sign * (t[1] * field[0]),
        )
    low = low_lanes(t[0].shape[0])
    turned = swap_halves(t[1])
    real = jnp.where(low, t[1], turned)
    imag = jnp.where(low, -turned, t[1])
    return (
        t[0] * field[0] - sign * (t[2] * field[2]),
        real * field[1] + sign * (imag * swap_halves(field[1])),
        t[0] * field[2] + sign * (t[2] * field[0]),
    )


def with_quarter_turn(parts):
    if len(parts) == 2:
        crossed = (-parts[1], parts[0])
    else:
        low = low_lanes(parts[1].shape[0])
        turned = swap_halves(parts[1])
        crossed = (-parts[2], jnp.where(low, -turned, turned), parts[0])
    both = [jnp.concatenate(rows, axis=1) for rows in (parts, crossed)]
    return jnp.concatenate(both, axis=0).astype(BF16)


def phases(dims):
    phase_rows, y_count = dims
    each = y_count // len(phase_rows)
    for at, rows in enumerate(phase_rows):
        skip = (phase_rows[0] - rows) // 2
        yield at, at * each, each, skip, rows, at < len(phase_rows) // 2


def narrow_state(state, skip, rows):
    here = slice(skip, skip + rows)
    real, imag = narrowed(parts_of(state[here].astype(F32)))
    state[here, :LANES] = real.astype(state.dtype)
    state[here, LANES : 2 * LANES] = imag.astype(state.dtype)


def layer_parts(layer, core, reach, skip, rows, wide):
    at = pl.multiple_of(core * reach + skip, 16)
    parts = parts_of(layer[pl.ds(at, rows)].astype(F32))
    return parts if wide else narrowed(parts)


def forward_body(dims, *refs):
    band, phase_rows = dims
    count = len(phase_rows)
    row_mats, col_mats = refs[:count], refs[count : count + 2]
    own, halo, o_own, o_halo, kept, seed, psi, layer, goal, wave = refs[count + 2 :]
    core = lax.axis_index("core")
    strip = TAIL // 2
    total = phase_rows[0]
    own_rows = own.shape[0] * band // CORES
    head = (total - own_rows) // 2
    reach = halo.shape[0] * band
    y_count = own.shape[1]
    upper = lax.broadcasted_iota(jnp.int32, (TAIL, 3 * LANES), 0) < strip

    def tails(part, index, pair):
        one = part[index, 2 * pair, band:].astype(F32)
        two = part[index, 2 * pair + 1, band:].astype(F32)
        return one, two

    for part, base in ((own, reach), (halo, core * (reach + own.shape[0] * band))):
        for index in range(part.shape[0]):
            for pair in range(y_count // 2):
                one, two = tails(part, index, pair)
                at = base + index * band + pair * TAIL
                at = at if part is own else pl.multiple_of(at, TAIL)
                wave[pl.ds(at, TAIL)] = jnp.where(upper, one, pltpu.roll(two, strip, 0))
    psi[...] = wave[pl.ds(pl.multiple_of(core * reach, band), total)]
    for index in range(own.shape[0] // CORES):
        for pair in range(y_count // 2):
            one, two = tails(own, core * (own.shape[0] // CORES) + index, pair)
            both = jnp.where(upper, pltpu.roll(one, strip, 0), two)[:, :LANES]
            at = index * band + pair * TAIL
            goal[at : at + TAIL] = both + swap_halves(both)

    for phase, y_first, each, skip, rows, wide in phases((phase_rows, y_count)):
        lanes = (3 if wide else 2) * LANES
        here = slice(skip, skip + rows)
        mine_rows = slice(head - skip, head - skip + own_rows)
        if phase == count // 2:
            narrow_state(psi, skip, rows)

        def two_slices(step, _):
            y = y_first + step
            for parity in range(CORES):
                mine = core == parity
                pl.when(mine)(lambda: fill_layer(layer, own, halo, y, band, core))
                pl.when(jnp.logical_not(mine))(
                    lambda: fill_layer(layer, o_own, o_halo, y, band, core)
                )
                t = layer_parts(layer, core, reach, skip, rows, wide)
                product = times(t, parts_of(psi[here, :lanes]), False)
                inner = [part[mine_rows] for part in product]
                kept[CORES * y + parity] = own_columns(inner, own_rows).astype(BF16)
                field = with_quarter_turn(product)
                spread = jnp.dot(row_mats[phase][...], field, preferred_element_type=F32)
                col_mat = col_mats[0 if wide else 1][...]
                psi[here, :lanes] = jnp.dot(
                    spread.astype(BF16), col_mat, preferred_element_type=F32
                )
            return 0

        lax.fori_loop(0, each, two_slices, 0)
    wave_out = own_columns(parts_of(psi[head : head + own_rows, : 2 * LANES]), own_rows)
    square = wave_out * wave_out
    residual = square + swap_halves(square) - goal[...]
    seed[...] = (2.0 * residual * wave_out).astype(BF16)


def backward_body(dims, *refs):
    band, phase_rows = dims
    count = len(phase_rows)
    row_mats, col_mats = refs[:count], refs[count : count + 2]
    own, halo, o_own, o_halo, kept, seeds, left, right = refs[count + 2 : count + 10]
    terms, o_terms, field, layer = refs[count + 10 :]
    core = lax.axis_index("core")
    own_rows = own.shape[0] * band // CORES
    head = (phase_rows[0] - own_rows) // 2
    reach = halo.shape[0] * band
    y_count = own.shape[1]
    low = low_lanes(phase_rows[0])
    low_own = low_lanes(own_rows)
    middle = seeds[...].astype(F32)
    beside = left[...].astype(F32)
    field[:, :LANES] = jnp.where(low, beside, swap_halves(middle)).astype(BF16)
    field[:, LANES : 2 * LANES] = right[...]
    field[:, 2 * LANES :] = jnp.where(low, swap_halves(beside), middle).astype(BF16)

    for phase, y_first, each, skip, rows, wide in phases((phase_rows, y_count)):
        lanes = (3 if wide else 2) * LANES
        here = slice(skip, skip + rows)
        mine_rows = slice(head - skip, head - skip + own_rows)
        if phase == count // 2:
            narrow_state(field, skip, rows)

        def two_slices(step, _):
            y = y_count - 1 - y_first - step
            for parity in reversed(range(CORES)):
                mine = core == parity
                other = jnp.logical_not(mine)
                pl.when(mine)(lambda: fill_layer(layer, own, halo, y, band, core))
                pl.when(other)(lambda: fill_layer(layer, o_own, o_halo, y, band, core))
                col_mat = col_mats[0 if wide else 1][...]
                spread = jnp.dot(field[here, :lanes], col_mat, preferred_element_type=F32)
                both = with_quarter_turn(parts_of(spread))
                back = parts_of(
                    jnp.dot(row_mats[phase][...], both, preferred_element_type=F32)
                )
                u = kept[CORES * y + parity].astype(F32)
                v = own_columns([part[mine_rows] for part in back], own_rows)
                u_turn, v_turn = swap_halves(u), swap_halves(v)
                phase_term = u * v_turn - u_turn * v
                term = jnp.where(low_own, phase_term, -(u * v + u_turn * v_turn)).astype(BF16)

                def put(out):
                    for index in range(out.shape[0]):
                        out[index, y] = term[index * band : (index + 1) * band]

                pl.when(mine)(lambda: put(terms))
                pl.when(other)(lambda: put(o_terms))
                t = layer_parts(layer, core, reach, skip, rows, wide)
                earlier = times(t, back, True)
                field[here, :lanes] = jnp.concatenate(earlier, axis=1).astype(BF16)
            return 0

        lax.fori_loop(0, each, two_slices, 0)


def collect_body(dims, offsets, terms, gradient):
    probes, tiles, y_count, lat_count, window, columns = dims
    band = terms.shape[1]
    lat = lax.axis_index("z") * GROUP + lax.axis_index("x")
    slots = {}
    for spot in range(y_count * GROUP):
        slots[tile_at(spot // y_count, spot % y_count, y_count, probes)] = spot
    low = low_lanes(band)
    rest = jnp.zeros((band, columns - window), F32)
    moved = []
    for probe in range(probes):
        parts = ([], [])
        for pair in range(tiles // 2):
            one = terms[slots[probe, 2 * pair]].astype(F32)
            two = terms[slots[probe, 2 * pair + 1]].astype(F32)
            parts[0].append(jnp.where(low, one, swap_halves(two)))
            parts[1].append(jnp.where(low, swap_halves(one), two))
        half = half_of(offsets, probe, band, lat, lat_count)
        for part in range(2):
            row = pltpu.roll(jnp.concatenate(parts[part] + [rest], axis=1), offsets[probe, 1], 1)
            moved.append((part, half, row))
    for part in range(2):
        for at in range(2):
            total = jnp.zeros((band, columns), F32)
            for which, half, row in moved:
                if which == part:
                    total = total + jnp.where(half == at, row, 0.0)
            gradient[part, at] = total


def local(potential, incident, measured, offsets, kernel):
    y_count = lax.axis_size("y")
    z_count = lax.axis_size("z")
    lat_count = z_count * GROUP
    band = potential.shape[3]
    columns = potential.shape[4]
    window = incident.shape[3]
    probes = incident.shape[1]
    half_width = (kernel.shape[1] - 1) // 2
    slices = y_count * CORES
    halo = slices * half_width
    tiles = y_count * GROUP // probes
    spots = y_count * GROUP
    reach = halo // band
    own_rows = GROUP // CORES * band
    phase_rows = tuple(own_rows + 2 * halo - at for at in range(0, 2 * halo, band))
    lanes = 3 * LANES
    taps = kernel.astype(F32).reshape(-1)
    core = lax.axis_index("core")

    def shape(*dims, dtype=BF16):
        return jax.ShapeDtypeStruct(dims, dtype)

    sent = call(
        functools.partial(prepare_body, (probes, tiles, halo, y_count, lat_count)),
        shape(spots, band + TAIL, lanes),
        [offsets],
        [potential[:, 0], incident, measured],
        (20_000_000, 3_000_000),
        [
            pltpu.VMEM((probes, 2, band, columns), F32),
            pltpu.VMEM((2, probes, TAIL, window), F32),
            pltpu.VMEM((probes, TAIL, window), F32),
            pltpu.SemaphoreType.DMA((probes + 2,)),
        ],
        outside=3,
        grant=WIDE_BYTES,
    )
    row_shapes = tuple(shape(rows, 2 * rows) for rows in phase_rows)
    col_shapes = (shape(lanes, lanes), shape(2 * LANES, 2 * LANES))
    matrices = call(
        functools.partial(
            matrices_body, (band, half_width, y_count, probes, lat_count, reach, phase_rows)
        ),
        row_shapes + row_shapes + col_shapes + col_shapes,
        [offsets, taps],
        [],
        (20_000_000, 1_500_000),
    )

    def spot_of(z, at_core):
        return at_core * z_count + z % z_count

    steps_z = range(z_count)
    same = [(spot_of(i, 0), spot_of(i + 1, 0)) for i in steps_z]
    same += [(spot_of(i + 1, 1), spot_of(i, 1)) for i in steps_z]
    cross = [(spot_of(i, 1), spot_of(i + 1, 0)) for i in steps_z]
    cross += [(spot_of(i + 1, 0), spot_of(i, 1)) for i in steps_z]

    def other_core(cells):
        return lax.ppermute(cells, "core", [(i, CORES - 1 - i) for i in range(CORES)])

    own = lax.all_to_all(sent, ("x", "y"), 0, 0, tiled=False)
    own = own.reshape(GROUP, y_count, band + TAIL, lanes)
    last_for_zero = lax.dynamic_slice_in_dim(own, (GROUP - reach) * (1 - core), reach, 0)
    last_for_one = lax.dynamic_slice_in_dim(own, (GROUP - reach) * core, reach, 0)
    edge = lax.ppermute(last_for_zero, ("core", "z"), same)
    o_edge = lax.ppermute(last_for_one, ("core", "z"), cross)
    o_own = other_core(own)
    edge, o_edge, o_own, *matrices = lax.optimization_barrier((edge, o_edge, o_own, *matrices))
    layers = (own, edge, o_own, o_edge)
    count = len(phase_rows)
    forward_mats = matrices[:count] + matrices[2 * count : 2 * count + 2]
    backward_mats = matrices[count : 2 * count] + matrices[2 * count + 2 :]

    flops = slices * phase_rows[1] * lanes * (4 * phase_rows[1] + 2 * lanes)
    kept, seed = call(
        functools.partial(forward_body, (band, phase_rows)),
        (shape(slices, own_rows, LANES), shape(own_rows, LANES)),
        [],
        [*forward_mats, *layers],
        (flops, 6_000_000),
        [
            pltpu.VMEM((phase_rows[0], lanes), F32),
            pltpu.VMEM(((GROUP + 2 * reach) * band, lanes), BF16),
            pltpu.VMEM((own_rows, LANES), F32),
            pltpu.VMEM(((GROUP + 2 * reach) * band, lanes), F32),
        ],
    )
    beyond = lax.ppermute(seed, ("core", "z"), cross)
    beside = other_core(seed)
    first_core = core == 0
    seeds = jnp.concatenate(
        [jnp.where(first_core, beyond, beside), seed, jnp.where(first_core, beside, beyond)],
        axis=0,
    )
    at = {}
    for y in range(y_count):
        for x in range(GROUP):
            at[tile_at(x, y, y_count, probes)] = y * GROUP + x
    right = [(at[p, c], at[p, c + 1]) for p in range(probes) for c in range(tiles - 1)]
    from_left = lax.ppermute(seeds, ("y", "x"), right)
    from_right = lax.ppermute(seeds, ("y", "x"), [(b, a) for a, b in right])
    terms, o_terms = call(
        functools.partial(backward_body, (band, phase_rows)),
        (
            shape(GROUP // CORES, y_count, band, LANES),
            shape(GROUP // CORES, y_count, band, LANES),
        ),
        [],
        [*backward_mats, *layers, kept, seeds, from_left, from_right],
        (flops, 6_000_000),
        [
            pltpu.VMEM((phase_rows[0], lanes), BF16),
            pltpu.VMEM(((GROUP + 2 * reach) * band, lanes), BF16),
        ],
    )
    o_terms = other_core(o_terms)
    terms = jnp.concatenate(
        [jnp.where(first_core, terms, o_terms), jnp.where(first_core, o_terms, terms)], axis=0
    )
    gathered = lax.all_to_all(
        terms.reshape(spots, band, LANES), ("x", "y"), 0, 0, tiled=False
    )
    gradient = call(
        functools.partial(collect_body, (probes, tiles, y_count, lat_count, window, columns)),
        shape(2, 2, band, columns, dtype=F32),
        [offsets],
        [gathered],
        (1_000_000, 2_000_000),
    )
    return gradient[:, None]


def solution(mesh):
    depth_count, lat_count = mesh.devices.shape
    grid = mesh.devices.reshape(depth_count // CORES, CORES, lat_count // GROUP, GROUP)
    fine = Mesh(grid, ("y", "core", "z", "x"))
    depth, lat = ("y", "core"), ("z", "x")
    in_specs = (
        P(None, depth, None, lat, None),
        P(None, None, lat, None),
        P(None, lat, None),
        P(),
        P(),
    )
    out_specs = P(None, depth, None, lat, None)
    return jax.shard_map(local, mesh=fine, in_specs=in_specs, out_specs=out_specs, check_vma=False)
```

```python
import functools

import jax
import jax.numpy as jnp
from jax import lax
from jax.experimental import pallas as pl
from jax.experimental.pallas import tpu as pltpu
from jax.sharding import Mesh
from jax.sharding import PartitionSpec as P

F32 = jnp.float32
BF16 = jnp.bfloat16
LANES = 128
PIECE = 64
CORES = 2
GROUP = 4
TAIL = 8
VMEM_BYTES = 16 * 1024 * 1024
WIDE_BYTES = 60 * 1024 * 1024


def vmem_spec():
    return pl.BlockSpec(memory_space=pltpu.VMEM)


def smem_spec():
    return pl.BlockSpec(memory_space=pltpu.SMEM)


def call(body, outs, scalars, arrays, cost, scratch=(), outside=0, grant=VMEM_BYTES):
    in_specs = [smem_spec()] * len(scalars)
    in_specs += [pl.BlockSpec(memory_space=pltpu.HBM)] * outside
    in_specs += [vmem_spec()] * (len(arrays) - outside)
    return pl.pallas_call(
        body,
        out_shape=outs,
        in_specs=in_specs,
        out_specs=jax.tree.map(lambda _: vmem_spec(), outs),
        scratch_shapes=list(scratch),
        compiler_params=pltpu.CompilerParams(vmem_limit_bytes=grant),
        cost_estimate=pl.CostEstimate(flops=cost[0], bytes_accessed=cost[1], transcendentals=0),
    )(*scalars, *arrays)


def tile_at(x, y, y_count, probes):
    rows = y_count // probes
    probe, row = y // rows, y % rows
    return probe, row * GROUP + (x if row % 2 == 0 else GROUP - 1 - x)


def low_lanes(rows):
    return lax.broadcasted_iota(jnp.int32, (rows, LANES), 1) < PIECE


def swap_halves(cells):
    return pltpu.roll(cells, PIECE, 1)


def half_of(offsets, probe, band, lat, lat_count):
    first = offsets[probe, 0] // band
    return (first + lax.rem(lat - first + lat_count, lat_count)) // lat_count


def packed(real, imag, tiles):
    span = real.shape[1]
    real_on = pltpu.roll(real, span - PIECE, 1)
    imag_on = pltpu.roll(imag, span - PIECE, 1)
    low = low_lanes(real.shape[0])
    out = []
    for tile in range(tiles):
        base = tile // 2 * LANES
        here, there = slice(base, base + LANES), slice(base + LANES, base + 2 * LANES)
        if tile % 2 == 0:
            middle = jnp.where(low, real[:, there], imag_on[:, here])
            out.append((real[:, here], middle, imag[:, here]))
        else:
            middle = jnp.where(low, real_on[:, there], imag[:, there])
            out.append((real_on[:, here], middle, imag_on[:, here]))
    return out


def cos_sin(phase):
    half = 0.5 * phase
    square = half * half
    sin, cos = 1.0 / 6227020800.0, 1.0 / 479001600.0
    for term in (-39916800.0, 362880.0, -5040.0, 120.0, -6.0, 1.0):
        sin = sin * square + 1.0 / term
    for term in (-3628800.0, 40320.0, -720.0, 24.0, -2.0, 1.0):
        cos = cos * square + 1.0 / term
    sin = sin * half
    return 1.0 - 2.0 * (sin * sin), 2.0 * (sin * cos)


def prepare_body(
    dims, offsets, potential, incident, measured, sent, pot_buf, inc_buf, mea_buf, sems
):
    probes, tiles, halo, y_count, lat_count = dims
    band, columns = pot_buf.shape[2], pot_buf.shape[3]
    window = inc_buf.shape[3]
    span = window + 2 * halo
    y = lax.axis_index("y")
    lat = lax.axis_index("z") * GROUP + lax.axis_index("x")
    strip = TAIL // 2
    first = pl.multiple_of(y // 2 * TAIL, TAIL)
    copies = []
    for probe in range(probes):
        half = half_of(offsets, probe, band, lat, lat_count)
        copies.append(
            pltpu.make_async_copy(potential.at[:, half], pot_buf.at[probe], sems.at[probe])
        )
    copies.append(
        pltpu.make_async_copy(incident.at[:, :, pl.ds(first, TAIL)], inc_buf, sems.at[probes])
    )
    copies.append(
        pltpu.make_async_copy(measured.at[:, pl.ds(first, TAIL)], mea_buf, sems.at[probes + 1])
    )
    for copy in copies:
        copy.start()
    slots = {}
    for spot in range(y_count * GROUP):
        slots[tile_at(spot // y_count, spot % y_count, y_count, probes)] = spot
    lane = lax.broadcasted_iota(jnp.int32, (band, span), 1)
    inside = (lane >= halo) & (lane < window + halo)
    for probe in range(probes):
        copies[probe].wait()
        turn = lax.rem(columns + halo - offsets[probe, 1], columns)
        phase = pltpu.roll(pot_buf[probe, 0], turn, 1)[:, :span]
        absorb = pltpu.roll(pot_buf[probe, 1], turn, 1)[:, :span]
        damping = jnp.where(inside, jnp.exp(-absorb), 0.0)
        cos, sin = cos_sin(phase)
        for tile, parts in enumerate(packed(damping * cos, damping * sin, tiles)):
            for at, part in enumerate(parts):
                cols = slice(at * LANES, (at + 1) * LANES)
                sent[slots[probe, tile], :band, cols] = part.astype(BF16)
    copies[probes].wait()
    copies[probes + 1].wait()
    odd = lax.rem(y, 2) == 1
    rest = jnp.zeros((TAIL, 2 * halo), F32)
    upper = lax.broadcasted_iota(jnp.int32, (TAIL, LANES), 0) < strip
    low = low_lanes(TAIL)
    for probe in range(probes):
        wide = []
        for part in range(2):
            rows = inc_buf[part, probe]
            rows = jnp.where(odd, pltpu.roll(rows, strip, 0), rows)
            wide.append(pltpu.roll(jnp.concatenate([rows, rest], axis=1), halo, 1))
        rows = mea_buf[probe]
        rows = jnp.where(odd, rows, pltpu.roll(rows, strip, 0))
        coarse = rows.astype(BF16).astype(F32)
        fine = rows - coarse
        coarse_on = pltpu.roll(coarse, window - PIECE, 1)
        fine_back = pltpu.roll(fine, PIECE, 1)
        for tile, parts in enumerate(packed(wide[0], wide[1], tiles)):
            here = slice(tile // 2 * LANES, tile // 2 * LANES + LANES)
            if tile % 2 == 0:
                both = jnp.where(low, coarse[:, here], fine_back[:, here])
            else:
                both = jnp.where(low, coarse_on[:, here], fine[:, here])
            for at, part in enumerate(parts):
                cols = slice(at * LANES, (at + 1) * LANES)
                under = both if at == 0 else jnp.zeros_like(both)
                sent[slots[probe, tile], band:, cols] = jnp.where(upper, part, under).astype(BF16)


def banded(taps, diff, half_width, conj):
    count = 2 * half_width + 1
    real = jnp.zeros(diff.shape, F32)
    imag = jnp.zeros(diff.shape, F32)
    for tap in range(count):
        hit = diff == tap - half_width
        source = count - 1 - tap if conj else tap
        real = jnp.where(hit, taps[source], real)
        value = taps[count + source]
        imag = jnp.where(hit, -value if conj else value, imag)
    return real, imag


def matrices_body(dims, conj, offsets, taps, *outs):
    band, half_width, y_count, probes, lat_count, reach, phase_rows = dims
    own = lax.axis_index("y") // (y_count // probes)
    start = lax.axis_index("z") * GROUP + lax.axis_index("core") * (GROUP // CORES) - reach
    base = lax.rem(start - offsets[own, 0] // band + 2 * lat_count, lat_count)

    def window_row(rows, axis):
        skip = (phase_rows[0] - rows) // 2
        index = lax.broadcasted_iota(jnp.int32, (rows, rows), axis) + skip
        at = index + base * band
        return jnp.where(at >= lat_count * band, at - lat_count * band, at)

    def column(lanes, axis):
        index = lax.broadcasted_iota(jnp.int32, (lanes, lanes), axis)
        if lanes == 2 * LANES:
            return jnp.where(index >= LANES, index - LANES, index), index >= LANES
        imag = index >= LANES + PIECE
        inner = jnp.where(imag, index - PIECE, index)
        return jnp.where(index >= 2 * LANES, index - 2 * LANES, inner), imag

    count = len(phase_rows)
    for out, rows in zip(outs[:count], phase_rows):
        diff = window_row(rows, 1) - window_row(rows, 0)
        real, imag = banded(taps, diff, half_width, conj)
        out[...] = jnp.concatenate([real, imag], axis=1).astype(BF16)
    for out in outs[count:]:
        in_col, in_imag = column(out.shape[0], 0)
        out_col, out_imag = column(out.shape[0], 1)
        real, imag = banded(taps, in_col - out_col, half_width, conj)
        signed = jnp.where(in_imag, -imag, imag)
        out[...] = jnp.where(in_imag == out_imag, real, signed).astype(BF16)


def parts_of(cells):
    return tuple(cells[:, at : at + LANES] for at in range(0, cells.shape[1], LANES))


def fill_layers(layers, sources, y, band, core):
    for parity, (own, halo) in ((core, sources[:2]), (CORES - 1 - core, sources[2:])):
        reach = halo.shape[0] * band
        for index in range(own.shape[0]):
            rows = slice(reach + index * band, reach + (index + 1) * band)
            layers[CORES * y + parity, rows] = own[index, y, :band]
        base = core * (reach + own.shape[0] * band)
        for index in range(halo.shape[0]):
            rows = pl.ds(pl.multiple_of(base + index * band, band), band)
            layers[CORES * y + parity, rows] = halo[index, y, :band]


def narrowed(wide):
    first, middle, last = wide
    edge = lax.broadcasted_iota(jnp.int32, first.shape, 1) < LANES - PIECE // 2
    on, back = LANES - PIECE // 2, PIECE // 2
    real = jnp.where(edge, pltpu.roll(first, on, 1), pltpu.roll(middle, on, 1))
    imag = jnp.where(edge, pltpu.roll(last, on, 1), pltpu.roll(middle, back, 1))
    return real, imag


def own_columns(parts, rows):
    low = low_lanes(rows)
    if len(parts) == 3:
        return jnp.where(low, swap_halves(parts[0]), parts[2])
    real = pltpu.roll(parts[0], LANES - PIECE // 2, 1)
    return jnp.where(low, real, pltpu.roll(parts[1], PIECE // 2, 1))


def times(t, field, conj):
    sign = -1.0 if conj else 1.0
    if len(t) == 2:
        return (
            t[0] * field[0] - sign * (t[1] * field[1]),
            t[0] * field[1] + sign * (t[1] * field[0]),
        )
    low = low_lanes(t[0].shape[0])
    turned = swap_halves(t[1])
    real = jnp.where(low, t[1], turned)
    imag = jnp.where(low, -turned, t[1])
    return (
        t[0] * field[0] - sign * (t[2] * field[2]),
        real * field[1] + sign * (imag * swap_halves(field[1])),
        t[0] * field[2] + sign * (t[2] * field[0]),
    )


def with_quarter_turn(parts):
    if len(parts) == 2:
        crossed = (-parts[1], parts[0])
    else:
        low = low_lanes(parts[1].shape[0])
        turned = swap_halves(parts[1])
        crossed = (-parts[2], jnp.where(low, -turned, turned), parts[0])
    both = [jnp.concatenate(rows, axis=1) for rows in (parts, crossed)]
    return jnp.concatenate(both, axis=0).astype(BF16)


def phases(dims):
    phase_rows, y_count = dims
    each = y_count // len(phase_rows)
    for at, rows in enumerate(phase_rows):
        skip = (phase_rows[0] - rows) // 2
        yield at, at * each, each, skip, rows, at < len(phase_rows) // 2


def narrow_state(state, skip, rows):
    here = slice(skip, skip + rows)
    real, imag = narrowed(parts_of(state[here].astype(F32)))
    state[here, :LANES] = real.astype(state.dtype)
    state[here, LANES : 2 * LANES] = imag.astype(state.dtype)


def layer_parts(layers, index, core, reach, skip, rows, wide):
    at = pl.multiple_of(core * reach + skip, 16)
    parts = parts_of(layers[index, pl.ds(at, rows)].astype(F32))
    return parts if wide else narrowed(parts)


def forward_body(dims, *refs):
    band, phase_rows = dims
    count = len(phase_rows)
    row_mats, col_mats = refs[:count], refs[count : count + 2]
    own, halo, o_own, o_halo, kept, seed, psi, layers, goal, wave = refs[count + 2 :]
    sources = (own, halo, o_own, o_halo)
    core = lax.axis_index("core")
    strip = TAIL // 2
    total = phase_rows[0]
    own_rows = own.shape[0] * band // CORES
    head = (total - own_rows) // 2
    reach = halo.shape[0] * band
    y_count = own.shape[1]
    upper = lax.broadcasted_iota(jnp.int32, (TAIL, 3 * LANES), 0) < strip

    def tails(part, index, pair):
        one = part[index, 2 * pair, band:].astype(F32)
        two = part[index, 2 * pair + 1, band:].astype(F32)
        return one, two

    for part, base in ((own, reach), (halo, core * (reach + own.shape[0] * band))):
        for index in range(part.shape[0]):
            for pair in range(y_count // 2):
                one, two = tails(part, index, pair)
                at = base + index * band + pair * TAIL
                at = at if part is own else pl.multiple_of(at, TAIL)
                wave[pl.ds(at, TAIL)] = jnp.where(upper, one, pltpu.roll(two, strip, 0))
    psi[...] = wave[pl.ds(pl.multiple_of(core * reach, band), total)]
    for index in range(own.shape[0] // CORES):
        for pair in range(y_count // 2):
            one, two = tails(own, core * (own.shape[0] // CORES) + index, pair)
            both = jnp.where(upper, pltpu.roll(one, strip, 0), two)[:, :LANES]
            at = index * band + pair * TAIL
            goal[at : at + TAIL] = both + swap_halves(both)

    fill_layers(layers, sources, 0, band, core)
    for phase, y_first, each, skip, rows, wide in phases((phase_rows, y_count)):
        lanes = (3 if wide else 2) * LANES
        here = slice(skip, skip + rows)
        mine_rows = slice(head - skip, head - skip + own_rows)
        if phase == count // 2:
            narrow_state(psi, skip, rows)

        def two_slices(step, _):
            y = y_first + step
            fill_layers(layers, sources, jnp.minimum(y + 1, y_count - 1), band, core)
            for parity in range(CORES):
                t = layer_parts(layers, CORES * y + parity, core, reach, skip, rows, wide)
                product = times(t, parts_of(psi[here, :lanes]), False)
                inner = [part[mine_rows] for part in product]
                kept[CORES * y + parity] = own_columns(inner, own_rows).astype(BF16)
                field = with_quarter_turn(product)
                spread = jnp.dot(row_mats[phase][...], field, preferred_element_type=F32)
                col_mat = col_mats[0 if wide else 1][...]
                psi[here, :lanes] = jnp.dot(
                    spread.astype(BF16), col_mat, preferred_element_type=F32
                )
            return 0

        lax.fori_loop(0, each, two_slices, 0)
    wave_out = own_columns(parts_of(psi[head : head + own_rows, : 2 * LANES]), own_rows)
    square = wave_out * wave_out
    residual = square + swap_halves(square) - goal[...]
    seed[...] = (2.0 * residual * wave_out).astype(BF16)


def backward_body(dims, *refs):
    band, phase_rows = dims
    count = len(phase_rows)
    row_mats, col_mats = refs[:count], refs[count : count + 2]
    own, halo, o_own, o_halo, kept, seeds, beside, beyond = refs[count + 2 : count + 10]
    terms, field, layers = refs[count + 10 :]
    sources = (own, halo, o_own, o_halo)
    core = lax.axis_index("core")
    own_rows = own.shape[0] * band // CORES
    head = (phase_rows[0] - own_rows) // 2
    reach = halo.shape[0] * band
    y_count = own.shape[1]
    low_own = low_lanes(own_rows)
    tail = phase_rows[0] - own_rows

    for part, base in ((seeds, head), (beside, (1 - core) * tail), (beyond, core * tail)):
        left, middle = part[0].astype(F32), part[1].astype(F32)
        rows = pl.ds(base if part is seeds else pl.multiple_of(base, band), own_rows)
        field[rows, :LANES] = jnp.where(low_own, left, swap_halves(middle)).astype(BF16)
        field[rows, LANES : 2 * LANES] = part[2]
        field[rows, 2 * LANES :] = jnp.where(low_own, swap_halves(left), middle).astype(BF16)

    fill_layers(layers, sources, y_count - 1, band, core)
    for phase, y_first, each, skip, rows, wide in phases((phase_rows, y_count)):
        lanes = (3 if wide else 2) * LANES
        here = slice(skip, skip + rows)
        mine_rows = slice(head - skip, head - skip + own_rows)
        if phase == count // 2:
            narrow_state(field, skip, rows)

        def two_slices(step, _):
            y = y_count - 1 - y_first - step
            fill_layers(layers, sources, jnp.maximum(y - 1, 0), band, core)
            for parity in reversed(range(CORES)):
                col_mat = col_mats[0 if wide else 1][...]
                spread = jnp.dot(field[here, :lanes], col_mat, preferred_element_type=F32)
                both = with_quarter_turn(parts_of(spread))
                back = parts_of(
                    jnp.dot(row_mats[phase][...], both, preferred_element_type=F32)
                )
                t = layer_parts(layers, CORES * y + parity, core, reach, skip, rows, wide)
                earlier = times(t, back, True)
                field[here, :lanes] = jnp.concatenate(earlier, axis=1).astype(BF16)
                u = kept[CORES * y + parity].astype(F32)
                v = own_columns([part[mine_rows] for part in back], own_rows)
                u_turn, v_turn = swap_halves(u), swap_halves(v)
                phase_term = u * v_turn - u_turn * v
                term = jnp.where(low_own, phase_term, -(u * v + u_turn * v_turn)).astype(BF16)
                owner = lax.rem(core + parity, CORES)
                for index in range(terms.shape[1]):
                    terms[owner, index, y] = term[index * band : (index + 1) * band]
            return 0

        lax.fori_loop(0, each, two_slices, 0)


def collect_body(dims, offsets, terms, gradient):
    probes, tiles, y_count, lat_count, window, columns = dims
    band = terms.shape[1]
    lat = lax.axis_index("z") * GROUP + lax.axis_index("x")
    slots = {}
    for spot in range(y_count * GROUP):
        slots[tile_at(spot // y_count, spot % y_count, y_count, probes)] = spot
    low = low_lanes(band)
    rest = jnp.zeros((band, columns - window), F32)
    moved = []
    for probe in range(probes):
        parts = ([], [])
        for pair in range(tiles // 2):
            one = terms[slots[probe, 2 * pair]].astype(F32)
            two = terms[slots[probe, 2 * pair + 1]].astype(F32)
            parts[0].append(jnp.where(low, one, swap_halves(two)))
            parts[1].append(jnp.where(low, swap_halves(one), two))
        half = half_of(offsets, probe, band, lat, lat_count)
        for part in range(2):
            row = pltpu.roll(jnp.concatenate(parts[part] + [rest], axis=1), offsets[probe, 1], 1)
            moved.append((part, half, row))
    for part in range(2):
        for at in range(2):
            total = jnp.zeros((band, columns), F32)
            for which, half, row in moved:
                if which == part:
                    total = total + jnp.where(half == at, row, 0.0)
            gradient[part, at] = total


def local(potential, incident, measured, offsets, kernel):
    y_count = lax.axis_size("y")
    z_count = lax.axis_size("z")
    lat_count = z_count * GROUP
    band = potential.shape[3]
    columns = potential.shape[4]
    window = incident.shape[3]
    probes = incident.shape[1]
    half_width = (kernel.shape[1] - 1) // 2
    slices = y_count * CORES
    halo = slices * half_width
    tiles = y_count * GROUP // probes
    spots = y_count * GROUP
    reach = halo // band
    own_rows = GROUP // CORES * band
    phase_rows = tuple(own_rows + 2 * halo - at for at in range(0, 2 * halo, band))
    lanes = 3 * LANES
    taps = kernel.astype(F32).reshape(-1)
    core = lax.axis_index("core")

    def shape(*dims, dtype=BF16):
        return jax.ShapeDtypeStruct(dims, dtype)

    sent = call(
        functools.partial(prepare_body, (probes, tiles, halo, y_count, lat_count)),
        shape(spots, band + TAIL, lanes),
        [offsets],
        [potential[:, 0], incident, measured],
        (20_000_000, 3_000_000),
        [
            pltpu.VMEM((probes, 2, band, columns), F32),
            pltpu.VMEM((2, probes, TAIL, window), F32),
            pltpu.VMEM((probes, TAIL, window), F32),
            pltpu.SemaphoreType.DMA((probes + 2,)),
        ],
        outside=3,
        grant=WIDE_BYTES,
    )
    mat_shapes = tuple(shape(rows, 2 * rows) for rows in phase_rows)
    mat_shapes += (shape(lanes, lanes), shape(2 * LANES, 2 * LANES))
    mat_dims = (band, half_width, y_count, probes, lat_count, reach, phase_rows)

    def matrices(conj, taps):
        body = functools.partial(matrices_body, mat_dims, conj)
        return call(body, mat_shapes, [offsets, taps], [], (20_000_000, 700_000))

    def spot_of(z, at_core):
        return at_core * z_count + z % z_count

    steps_z = range(z_count)
    same = [(spot_of(i, 0), spot_of(i + 1, 0)) for i in steps_z]
    same += [(spot_of(i + 1, 1), spot_of(i, 1)) for i in steps_z]
    cross = [(spot_of(i, 1), spot_of(i + 1, 0)) for i in steps_z]
    cross += [(spot_of(i + 1, 0), spot_of(i, 1)) for i in steps_z]

    def other_core(cells):
        return lax.ppermute(cells, "core", [(i, CORES - 1 - i) for i in range(CORES)])

    own = lax.all_to_all(sent, ("x", "y"), 0, 0, tiled=False)
    own = own.reshape(GROUP, y_count, band + TAIL, lanes)
    last_for_zero = lax.dynamic_slice_in_dim(own, (GROUP - reach) * (1 - core), reach, 0)
    last_for_one = lax.dynamic_slice_in_dim(own, (GROUP - reach) * core, reach, 0)
    edge = lax.ppermute(last_for_zero, ("core", "z"), same)
    o_edge = lax.ppermute(last_for_one, ("core", "z"), cross)
    o_own = other_core(own)
    edge, o_edge, o_own, *forward_mats = lax.optimization_barrier(
        (edge, o_edge, o_own, *matrices(False, taps))
    )
    layers = (own, edge, o_own, o_edge)

    flops = slices * phase_rows[1] * lanes * (4 * phase_rows[1] + 2 * lanes)
    kept, seed = call(
        functools.partial(forward_body, (band, phase_rows)),
        (shape(slices, own_rows, LANES), shape(own_rows, LANES)),
        [],
        [*forward_mats, *layers],
        (flops, 6_000_000),
        [
            pltpu.VMEM((phase_rows[0], lanes), F32),
            pltpu.VMEM((slices, (GROUP + 2 * reach) * band, lanes), BF16),
            pltpu.VMEM((own_rows, LANES), F32),
            pltpu.VMEM(((GROUP + 2 * reach) * band, lanes), F32),
        ],
    )
    at = {}
    for y in range(y_count):
        for x in range(GROUP):
            at[tile_at(x, y, y_count, probes)] = y * GROUP + x
    right = [(at[p, c], at[p, c + 1]) for p in range(probes) for c in range(tiles - 1)]
    seed, late_taps = lax.optimization_barrier((seed, taps))
    from_left = lax.ppermute(seed, ("y", "x"), right)
    from_right = lax.ppermute(seed, ("y", "x"), [(b, a) for a, b in right])
    from_left, from_right, *backward_mats = lax.optimization_barrier(
        (from_left, from_right, *matrices(True, late_taps))
    )
    seeds = jnp.stack([from_left, seed, from_right])
    beyond = lax.ppermute(seeds, ("core", "z"), cross)
    beside = other_core(seeds)
    terms = call(
        functools.partial(backward_body, (band, phase_rows)),
        shape(CORES, GROUP // CORES, y_count, band, LANES),
        [],
        [*backward_mats, *layers, kept, seeds, beside, beyond],
        (flops, 6_000_000),
        [
            pltpu.VMEM((phase_rows[0], lanes), BF16),
            pltpu.VMEM((slices, (GROUP + 2 * reach) * band, lanes), BF16),
        ],
    )
    mine, others = terms[0], other_core(terms[1])
    first_core = core == 0
    terms = jnp.concatenate(
        [jnp.where(first_core, mine, others), jnp.where(first_core, others, mine)], axis=0
    )
    gathered = lax.all_to_all(
        terms.reshape(spots, band, LANES), ("x", "y"), 0, 0, tiled=False
    )
    gradient = call(
        functools.partial(collect_body, (probes, tiles, y_count, lat_count, window, columns)),
        shape(2, 2, band, columns, dtype=F32),
        [offsets],
        [gathered],
        (1_000_000, 2_000_000),
    )
    return gradient[:, None]


def solution(mesh):
    depth_count, lat_count = mesh.devices.shape
    grid = mesh.devices.reshape(depth_count // CORES, CORES, lat_count // GROUP, GROUP)
    fine = Mesh(grid, ("y", "core", "z", "x"))
    depth, lat = ("y", "core"), ("z", "x")
    in_specs = (
        P(None, depth, None, lat, None),
        P(None, None, lat, None),
        P(None, lat, None),
        P(),
        P(),
    )
    out_specs = P(None, depth, None, lat, None)
    return jax.shard_map(local, mesh=fine, in_specs=in_specs, out_specs=out_specs, check_vma=False)
```

```python
import functools

import jax
import jax.numpy as jnp
from jax import lax
from jax.experimental import pallas as pl
from jax.experimental.pallas import tpu as pltpu
from jax.sharding import Mesh
from jax.sharding import PartitionSpec as P

F32 = jnp.float32
BF16 = jnp.bfloat16
LANES = 128
PIECE = 64
CORES = 2
GROUP = 4
TAIL = 8
STRIP = 2
VMEM_BYTES = 16 * 1024 * 1024
WIDE_BYTES = 60 * 1024 * 1024


def vmem_spec():
    return pl.BlockSpec(memory_space=pltpu.VMEM)


def smem_spec():
    return pl.BlockSpec(memory_space=pltpu.SMEM)


def call(body, outs, scalars, arrays, cost, scratch=(), outside=0, grant=VMEM_BYTES):
    in_specs = [smem_spec()] * len(scalars)
    in_specs += [pl.BlockSpec(memory_space=pltpu.HBM)] * outside
    in_specs += [vmem_spec()] * (len(arrays) - outside)
    return pl.pallas_call(
        body,
        out_shape=outs,
        in_specs=in_specs,
        out_specs=jax.tree.map(lambda _: vmem_spec(), outs),
        scratch_shapes=list(scratch),
        compiler_params=pltpu.CompilerParams(vmem_limit_bytes=grant),
        cost_estimate=pl.CostEstimate(flops=cost[0], bytes_accessed=cost[1], transcendentals=0),
    )(*scalars, *arrays)


def tile_at(x, y, y_count, probes):
    rows = y_count // probes
    probe, row = y // rows, y % rows
    return probe, row * GROUP + (x if row % 2 == 0 else GROUP - 1 - x)


def tile_slots(y_count, probes, core):
    slots = {}
    for x in range(GROUP):
        base = lax.rem(x + core * (GROUP // CORES), GROUP) * y_count
        for y in range(y_count):
            slots[tile_at(x, y, y_count, probes)] = base + y
    return slots


def low_lanes(rows):
    return lax.broadcasted_iota(jnp.int32, (rows, LANES), 1) < PIECE


def swap_halves(cells):
    return pltpu.roll(cells, PIECE, 1)


def half_of(offsets, probe, band, lat, lat_count):
    first = offsets[probe, 0] // band
    return (first + lax.rem(lat - first + lat_count, lat_count)) // lat_count


def packed(real, imag, tiles):
    span = real.shape[1]
    real_on = pltpu.roll(real, span - PIECE, 1)
    imag_on = pltpu.roll(imag, span - PIECE, 1)
    low = low_lanes(real.shape[0])
    out = []
    for tile in range(tiles):
        base = tile // 2 * LANES
        here, there = slice(base, base + LANES), slice(base + LANES, base + 2 * LANES)
        if tile % 2 == 0:
            middle = jnp.where(low, real[:, there], imag_on[:, here])
            out.append((real[:, here], middle, imag[:, here]))
        else:
            middle = jnp.where(low, real_on[:, there], imag[:, there])
            out.append((real_on[:, here], middle, imag_on[:, here]))
    return out


def cos_sin(phase):
    half = 0.5 * phase
    square = half * half
    sin, cos = 1.0 / 6227020800.0, 1.0 / 479001600.0
    for term in (-39916800.0, 362880.0, -5040.0, 120.0, -6.0, 1.0):
        sin = sin * square + 1.0 / term
    for term in (-3628800.0, 40320.0, -720.0, 24.0, -2.0, 1.0):
        cos = cos * square + 1.0 / term
    sin = sin * half
    return 1.0 - 2.0 * (sin * sin), 2.0 * (sin * cos)


def prepare_body(
    dims, offsets, potential, incident, measured, sent, pot_buf, inc_buf, mea_buf, sems
):
    probes, tiles, halo, y_count, lat_count = dims
    band, columns = pot_buf.shape[2], pot_buf.shape[3]
    window = inc_buf.shape[3]
    span = window + 2 * halo
    y, core = lax.axis_index("y"), lax.axis_index("core")
    lat = lax.axis_index("z") * GROUP + lax.axis_index("x")
    row = (y * CORES + core) * STRIP
    first = pl.multiple_of(row // TAIL * TAIL, TAIL)
    copies = []
    for probe in range(probes):
        half = half_of(offsets, probe, band, lat, lat_count)
        copies.append(
            pltpu.make_async_copy(potential.at[:, half], pot_buf.at[probe], sems.at[probe])
        )
    copies.append(
        pltpu.make_async_copy(incident.at[:, :, pl.ds(first, TAIL)], inc_buf, sems.at[probes])
    )
    copies.append(
        pltpu.make_async_copy(measured.at[:, pl.ds(first, TAIL)], mea_buf, sems.at[probes + 1])
    )
    for copy in copies:
        copy.start()
    slots = tile_slots(y_count, probes, core)
    lane = lax.broadcasted_iota(jnp.int32, (band, span), 1)
    inside = (lane >= halo) & (lane < window + halo)
    for probe in range(probes):
        copies[probe].wait()
        turn = lax.rem(columns + halo - offsets[probe, 1], columns)
        phase = pltpu.roll(pot_buf[probe, 0], turn, 1)[:, :span]
        absorb = pltpu.roll(pot_buf[probe, 1], turn, 1)[:, :span]
        damping = jnp.where(inside, jnp.exp(-absorb), 0.0)
        cos, sin = cos_sin(phase)
        for tile, parts in enumerate(packed(damping * cos, damping * sin, tiles)):
            for at, part in enumerate(parts):
                rows = slice(at * band, (at + 1) * band)
                sent[slots[probe, tile], rows] = part.astype(BF16)
    copies[probes].wait()
    copies[probes + 1].wait()
    lift = lax.rem(first + TAIL - row, TAIL)
    rest = jnp.zeros((TAIL, 2 * halo), F32)
    place = lax.broadcasted_iota(jnp.int32, (TAIL, LANES), 0) // STRIP
    low = low_lanes(TAIL)
    for probe in range(probes):
        wide = []
        for part in range(2):
            rows = pltpu.roll(inc_buf[part, probe], lift, 0)
            wide.append(pltpu.roll(jnp.concatenate([rows, rest], axis=1), halo, 1))
        rows = pltpu.roll(pltpu.roll(mea_buf[probe], lift, 0), 3 * STRIP, 0)
        coarse = rows.astype(BF16).astype(F32)
        fine = rows - coarse
        coarse_on = pltpu.roll(coarse, window - PIECE, 1)
        fine_back = pltpu.roll(fine, PIECE, 1)
        for tile, parts in enumerate(packed(wide[0], wide[1], tiles)):
            here = slice(tile // 2 * LANES, tile // 2 * LANES + LANES)
            if tile % 2 == 0:
                cells = jnp.where(low, coarse[:, here], fine_back[:, here])
            else:
                cells = jnp.where(low, coarse_on[:, here], fine[:, here])
            for at, part in enumerate(parts):
                moved = pltpu.roll(part, at * STRIP, 0) if at else part
                cells = jnp.where(place == at, moved, cells)
            sent[slots[probe, tile], 3 * band :] = cells.astype(BF16)


def banded(taps, diff, half_width, conj):
    count = 2 * half_width + 1
    real = jnp.zeros(diff.shape, F32)
    imag = jnp.zeros(diff.shape, F32)
    for tap in range(count):
        hit = diff == tap - half_width
        source = count - 1 - tap if conj else tap
        real = jnp.where(hit, taps[source], real)
        value = taps[count + source]
        imag = jnp.where(hit, -value if conj else value, imag)
    return real, imag


def matrices_body(dims, conj, offsets, taps, *outs):
    band, half_width, y_count, probes, lat_count, reach, phase_rows = dims
    own = lax.axis_index("y") // (y_count // probes)
    start = lax.axis_index("z") * GROUP + lax.axis_index("core") * (GROUP // CORES) - reach
    base = lax.rem(start - offsets[own, 0] // band + 2 * lat_count, lat_count)

    def window_row(rows, axis):
        skip = (phase_rows[0] - rows) // 2
        index = lax.broadcasted_iota(jnp.int32, (rows, rows), axis) + skip
        at = index + base * band
        return jnp.where(at >= lat_count * band, at - lat_count * band, at)

    def column(lanes, axis):
        index = lax.broadcasted_iota(jnp.int32, (lanes, lanes), axis)
        if lanes == 2 * LANES:
            return jnp.where(index >= LANES, index - LANES, index), index >= LANES
        imag = index >= LANES + PIECE
        inner = jnp.where(imag, index - PIECE, index)
        return jnp.where(index >= 2 * LANES, index - 2 * LANES, inner), imag

    count = len(phase_rows)
    for out, rows in zip(outs[:count], phase_rows):
        diff = window_row(rows, 1) - window_row(rows, 0)
        real, imag = banded(taps, diff, half_width, conj)
        out[...] = jnp.concatenate([real, imag], axis=1).astype(BF16)
    for out in outs[count:]:
        in_col, in_imag = column(out.shape[0], 0)
        out_col, out_imag = column(out.shape[0], 1)
        real, imag = banded(taps, in_col - out_col, half_width, conj)
        signed = jnp.where(in_imag, -imag, imag)
        out[...] = jnp.where(in_imag == out_imag, real, signed).astype(BF16)


def parts_of(cells):
    return tuple(cells[:, at : at + LANES] for at in range(0, cells.shape[1], LANES))


def band_rows(own, halo, band, core, index, of_other):
    reach = halo.shape[0] * band
    if index >= own.shape[0]:
        at = core * (reach + own.shape[0] * band) + (index - own.shape[0]) * band
    else:
        half = own.shape[0] // CORES
        later = core if (index < half) != of_other else CORES - 1 - core
        at = reach + (later * half + index % half) * band
    return pl.multiple_of(at, band)


def fill_layers(layers, sources, y, band, core):
    for of_other, (own, halo) in enumerate((sources[:2], sources[2:])):
        parity = CORES - 1 - core if of_other else core
        for index in range(own.shape[0] + halo.shape[0]):
            rows = pl.ds(band_rows(own, halo, band, core, index, bool(of_other)), band)
            inner = index - own.shape[0]
            cells = own[index, y, : 3 * band] if inner < 0 else halo[inner, y, : 3 * band]
            for at in range(3):
                cols = slice(at * LANES, (at + 1) * LANES)
                layers[CORES * y + parity, rows, cols] = cells[at * band : (at + 1) * band]


def narrowed(wide):
    first, middle, last = wide
    edge = lax.broadcasted_iota(jnp.int32, first.shape, 1) < LANES - PIECE // 2
    on, back = LANES - PIECE // 2, PIECE // 2
    real = jnp.where(edge, pltpu.roll(first, on, 1), pltpu.roll(middle, on, 1))
    imag = jnp.where(edge, pltpu.roll(last, on, 1), pltpu.roll(middle, back, 1))
    return real, imag


def own_columns(parts, rows):
    low = low_lanes(rows)
    if len(parts) == 3:
        return jnp.where(low, swap_halves(parts[0]), parts[2])
    real = pltpu.roll(parts[0], LANES - PIECE // 2, 1)
    return jnp.where(low, real, pltpu.roll(parts[1], PIECE // 2, 1))


def times(t, field, conj):
    sign = -1.0 if conj else 1.0
    if len(t) == 2:
        return (
            t[0] * field[0] - sign * (t[1] * field[1]),
            t[0] * field[1] + sign * (t[1] * field[0]),
        )
    low = low_lanes(t[0].shape[0])
    turned = swap_halves(t[1])
    real = jnp.where(low, t[1], turned)
    imag = jnp.where(low, -turned, t[1])
    return (
        t[0] * field[0] - sign * (t[2] * field[2]),
        real * field[1] + sign * (imag * swap_halves(field[1])),
        t[0] * field[2] + sign * (t[2] * field[0]),
    )


def with_quarter_turn(parts):
    if len(parts) == 2:
        crossed = (-parts[1], parts[0])
    else:
        low = low_lanes(parts[1].shape[0])
        turned = swap_halves(parts[1])
        crossed = (-parts[2], jnp.where(low, -turned, turned), parts[0])
    both = [jnp.concatenate(rows, axis=1) for rows in (parts, crossed)]
    return jnp.concatenate(both, axis=0).astype(BF16)


def phases(dims):
    phase_rows, y_count = dims
    each = y_count // len(phase_rows)
    for at, rows in enumerate(phase_rows):
        skip = (phase_rows[0] - rows) // 2
        yield at, at * each, each, skip, rows, at < len(phase_rows) // 2


def narrow_state(state, skip, rows):
    here = slice(skip, skip + rows)
    real, imag = narrowed(parts_of(state[here].astype(F32)))
    state[here, :LANES] = real.astype(state.dtype)
    state[here, LANES : 2 * LANES] = imag.astype(state.dtype)


def layer_parts(layers, index, core, reach, skip, rows, wide):
    at = pl.multiple_of(core * reach + skip, 16)
    parts = parts_of(layers[index, pl.ds(at, rows)].astype(F32))
    return parts if wide else narrowed(parts)


def forward_body(dims, *refs):
    band, phase_rows = dims
    count = len(phase_rows)
    row_mats, col_mats = refs[:count], refs[count : count + 2]
    own, halo, o_own, o_halo, kept, seed, psi, layers, goal, wave = refs[count + 2 :]
    sources = (own, halo, o_own, o_halo)
    core = lax.axis_index("core")
    total = phase_rows[0]
    own_rows = own.shape[0] * band // CORES
    head = (total - own_rows) // 2
    reach = halo.shape[0] * band
    y_count = own.shape[1]
    row = lax.broadcasted_iota(jnp.int32, (TAIL, LANES), 0)
    upper = row < TAIL // 2
    mine = lax.rem(row // STRIP, CORES) == core

    def both_strips(cells, o_cells):
        one = pltpu.roll(cells[3 * band :].astype(F32), STRIP * core, 0)
        two = pltpu.roll(o_cells[3 * band :].astype(F32), STRIP * (CORES - 1 - core), 0)
        return jnp.where(mine, one, two), jnp.where(mine, two, one)

    bands = own.shape[0] + halo.shape[0]
    for index in range(bands):
        base = band_rows(own, halo, band, core, index, False)
        for pair in range(y_count // 2):
            strips = []
            for y in (2 * pair, 2 * pair + 1):
                if index < own.shape[0]:
                    across = (index + own.shape[0] // CORES) % own.shape[0]
                    strips.append(both_strips(own[index, y], o_own[across, y]))
                else:
                    inner = index - own.shape[0]
                    strips.append(both_strips(halo[inner, y], o_halo[inner, y]))
            (even, even_mid), (odd, odd_mid) = strips
            rows = pl.ds(pl.multiple_of(base + pair * TAIL, TAIL), TAIL)
            turn = TAIL // 2
            wave[rows, :LANES] = jnp.where(upper, even, pltpu.roll(odd, turn, 0))
            wave[rows, LANES : 2 * LANES] = jnp.where(
                upper, pltpu.roll(even_mid, TAIL - STRIP, 0), pltpu.roll(odd_mid, STRIP, 0)
            )
            wave[rows, 2 * LANES :] = jnp.where(upper, pltpu.roll(even, turn, 0), odd)
            if index < own.shape[0] // CORES:
                both = jnp.where(
                    upper, pltpu.roll(even_mid, STRIP, 0), pltpu.roll(odd_mid, TAIL - STRIP, 0)
                )
                at = index * band + pair * TAIL
                goal[at : at + TAIL] = both + swap_halves(both)
    psi[...] = wave[pl.ds(pl.multiple_of(core * reach, band), total)]

    fill_layers(layers, sources, 0, band, core)
    for phase, y_first, each, skip, rows, wide in phases((phase_rows, y_count)):
        lanes = (3 if wide else 2) * LANES
        here = slice(skip, skip + rows)
        mine_rows = slice(head - skip, head - skip + own_rows)
        if phase == count // 2:
            narrow_state(psi, skip, rows)

        def two_slices(step, _):
            y = y_first + step
            fill_layers(layers, sources, jnp.minimum(y + 1, y_count - 1), band, core)
            for parity in range(CORES):
                t = layer_parts(layers, CORES * y + parity, core, reach, skip, rows, wide)
                product = times(t, parts_of(psi[here, :lanes]), False)
                inner = [part[mine_rows] for part in product]
                kept[CORES * y + parity] = own_columns(inner, own_rows).astype(BF16)
                field = with_quarter_turn(product)
                spread = jnp.dot(row_mats[phase][...], field, preferred_element_type=F32)
                col_mat = col_mats[0 if wide else 1][...]
                psi[here, :lanes] = jnp.dot(
                    spread.astype(BF16), col_mat, preferred_element_type=F32
                )
            return 0

        lax.fori_loop(0, each, two_slices, 0)
    wave_out = own_columns(parts_of(psi[head : head + own_rows, : 2 * LANES]), own_rows)
    square = wave_out * wave_out
    residual = square + swap_halves(square) - goal[...]
    seed[...] = (2.0 * residual * wave_out).astype(BF16)


def backward_body(dims, *refs):
    band, phase_rows = dims
    count = len(phase_rows)
    row_mats, col_mats = refs[:count], refs[count : count + 2]
    own, halo, o_own, o_halo, kept, seeds, beside, beyond = refs[count + 2 : count + 10]
    terms, field, layers = refs[count + 10 :]
    sources = (own, halo, o_own, o_halo)
    core = lax.axis_index("core")
    own_rows = own.shape[0] * band // CORES
    head = (phase_rows[0] - own_rows) // 2
    reach = halo.shape[0] * band
    y_count = own.shape[1]
    low_own = low_lanes(own_rows)
    tail = phase_rows[0] - own_rows

    for part, base in ((seeds, head), (beside, (1 - core) * tail), (beyond, core * tail)):
        left, middle = part[0].astype(F32), part[1].astype(F32)
        rows = pl.ds(base if part is seeds else pl.multiple_of(base, band), own_rows)
        field[rows, :LANES] = jnp.where(low_own, left, swap_halves(middle)).astype(BF16)
        field[rows, LANES : 2 * LANES] = part[2]
        field[rows, 2 * LANES :] = jnp.where(low_own, swap_halves(left), middle).astype(BF16)

    fill_layers(layers, sources, y_count - 1, band, core)
    for phase, y_first, each, skip, rows, wide in phases((phase_rows, y_count)):
        lanes = (3 if wide else 2) * LANES
        here = slice(skip, skip + rows)
        mine_rows = slice(head - skip, head - skip + own_rows)
        if phase == count // 2:
            narrow_state(field, skip, rows)

        def two_slices(step, _):
            y = y_count - 1 - y_first - step
            fill_layers(layers, sources, jnp.maximum(y - 1, 0), band, core)
            for parity in reversed(range(CORES)):
                col_mat = col_mats[0 if wide else 1][...]
                spread = jnp.dot(field[here, :lanes], col_mat, preferred_element_type=F32)
                both = with_quarter_turn(parts_of(spread))
                back = parts_of(
                    jnp.dot(row_mats[phase][...], both, preferred_element_type=F32)
                )
                t = layer_parts(layers, CORES * y + parity, core, reach, skip, rows, wide)
                earlier = times(t, back, True)
                field[here, :lanes] = jnp.concatenate(earlier, axis=1).astype(BF16)
                u = kept[CORES * y + parity].astype(F32)
                v = own_columns([part[mine_rows] for part in back], own_rows)
                u_turn, v_turn = swap_halves(u), swap_halves(v)
                phase_term = u * v_turn - u_turn * v
                term = jnp.where(low_own, phase_term, -(u * v + u_turn * v_turn)).astype(BF16)
                owner = lax.rem(core + parity, CORES)
                for index in range(terms.shape[1]):
                    terms[owner, index, y] = term[index * band : (index + 1) * band]
            return 0

        lax.fori_loop(0, each, two_slices, 0)


def collect_body(dims, offsets, terms, gradient):
    probes, tiles, y_count, lat_count, window, columns = dims
    band = terms.shape[1]
    lat = lax.axis_index("z") * GROUP + lax.axis_index("x")
    slots = tile_slots(y_count, probes, lax.axis_index("core"))
    low = low_lanes(band)
    rest = jnp.zeros((band, columns - window), F32)
    moved = []
    for probe in range(probes):
        parts = ([], [])
        for pair in range(tiles // 2):
            one = terms[slots[probe, 2 * pair]].astype(F32)
            two = terms[slots[probe, 2 * pair + 1]].astype(F32)
            parts[0].append(jnp.where(low, one, swap_halves(two)))
            parts[1].append(jnp.where(low, swap_halves(one), two))
        half = half_of(offsets, probe, band, lat, lat_count)
        for part in range(2):
            row = pltpu.roll(jnp.concatenate(parts[part] + [rest], axis=1), offsets[probe, 1], 1)
            moved.append((part, half, row))
    for part in range(2):
        for at in range(2):
            total = jnp.zeros((band, columns), F32)
            for which, half, row in moved:
                if which == part:
                    total = total + jnp.where(half == at, row, 0.0)
            gradient[part, at] = total


def local(potential, incident, measured, offsets, kernel):
    y_count = lax.axis_size("y")
    z_count = lax.axis_size("z")
    lat_count = z_count * GROUP
    band = potential.shape[3]
    columns = potential.shape[4]
    window = incident.shape[3]
    probes = incident.shape[1]
    half_width = (kernel.shape[1] - 1) // 2
    slices = y_count * CORES
    halo = slices * half_width
    tiles = y_count * GROUP // probes
    spots = y_count * GROUP
    reach = halo // band
    own_rows = GROUP // CORES * band
    phase_rows = tuple(own_rows + 2 * halo - at for at in range(0, 2 * halo, band))
    lanes = 3 * LANES
    taps = kernel.astype(F32).reshape(-1)
    core = lax.axis_index("core")

    def shape(*dims, dtype=BF16):
        return jax.ShapeDtypeStruct(dims, dtype)

    sent = call(
        functools.partial(prepare_body, (probes, tiles, halo, y_count, lat_count)),
        shape(spots, 3 * band + TAIL, LANES),
        [offsets],
        [potential[:, 0], incident, measured],
        (20_000_000, 3_000_000),
        [
            pltpu.VMEM((probes, 2, band, columns), F32),
            pltpu.VMEM((2, probes, TAIL, window), F32),
            pltpu.VMEM((probes, TAIL, window), F32),
            pltpu.SemaphoreType.DMA((probes + 2,)),
        ],
        outside=3,
        grant=WIDE_BYTES,
    )
    mat_shapes = tuple(shape(rows, 2 * rows) for rows in phase_rows)
    mat_shapes += (shape(lanes, lanes), shape(2 * LANES, 2 * LANES))
    mat_dims = (band, half_width, y_count, probes, lat_count, reach, phase_rows)

    def matrices(conj, taps):
        body = functools.partial(matrices_body, mat_dims, conj)
        return call(body, mat_shapes, [offsets, taps], [], (20_000_000, 700_000))

    def spot_of(z, at_core):
        return at_core * z_count + z % z_count

    steps_z = range(z_count)
    same = [(spot_of(i, 0), spot_of(i + 1, 0)) for i in steps_z]
    same += [(spot_of(i + 1, 1), spot_of(i, 1)) for i in steps_z]
    cross = [(spot_of(i, 1), spot_of(i + 1, 0)) for i in steps_z]
    cross += [(spot_of(i + 1, 0), spot_of(i, 1)) for i in steps_z]

    def other_core(cells):
        return lax.ppermute(cells, "core", [(i, CORES - 1 - i) for i in range(CORES)])

    groups = []
    for at_core in range(CORES):
        for z in range(z_count):
            order = [(x + at_core * (GROUP // CORES)) % GROUP for x in range(GROUP)]
            groups.append(
                [
                    ((y * CORES + at_core) * z_count + z) * GROUP + x
                    for x in order
                    for y in range(y_count)
                ]
            )

    def exchange(blocks):
        axes = ("y", "core", "z", "x")
        return lax.all_to_all(blocks, axes, 0, 0, axis_index_groups=groups, tiled=False)

    own = exchange(sent).reshape(GROUP, y_count, 3 * band + TAIL, LANES)
    edge = lax.ppermute(own[GROUP - reach :], ("core", "z"), same)
    o_edge = lax.ppermute(own[:reach], ("core", "z"), cross)
    swapped, *forward_mats = lax.optimization_barrier((own, *matrices(False, taps)))
    o_own = other_core(swapped)
    edge, o_edge, o_own, *forward_mats = lax.optimization_barrier(
        (edge, o_edge, o_own, *forward_mats)
    )
    layers = (own, edge, o_own, o_edge)

    flops = slices * phase_rows[1] * lanes * (4 * phase_rows[1] + 2 * lanes)
    kept, seed = call(
        functools.partial(forward_body, (band, phase_rows)),
        (shape(slices, own_rows, LANES), shape(own_rows, LANES)),
        [],
        [*forward_mats, *layers],
        (flops, 6_000_000),
        [
            pltpu.VMEM((phase_rows[0], lanes), F32),
            pltpu.VMEM((slices, (GROUP + 2 * reach) * band, lanes), BF16),
            pltpu.VMEM((own_rows, LANES), F32),
            pltpu.VMEM(((GROUP + 2 * reach) * band, lanes), F32),
        ],
    )
    at = {}
    for y in range(y_count):
        for x in range(GROUP):
            at[tile_at(x, y, y_count, probes)] = y * GROUP + x
    right = [(at[p, c], at[p, c + 1]) for p in range(probes) for c in range(tiles - 1)]
    seed, late_taps = lax.optimization_barrier((seed, taps))
    from_left = lax.ppermute(seed, ("y", "x"), right)
    from_right = lax.ppermute(seed, ("y", "x"), [(b, a) for a, b in right])
    from_left, from_right, *backward_mats = lax.optimization_barrier(
        (from_left, from_right, *matrices(True, late_taps))
    )
    seeds = jnp.stack([from_left, seed, from_right])
    beyond = lax.ppermute(seeds, ("core", "z"), cross)
    beside = other_core(seeds)
    terms = call(
        functools.partial(backward_body, (band, phase_rows)),
        shape(CORES, GROUP // CORES, y_count, band, LANES),
        [],
        [*backward_mats, *layers, kept, seeds, beside, beyond],
        (flops, 6_000_000),
        [
            pltpu.VMEM((phase_rows[0], lanes), BF16),
            pltpu.VMEM((slices, (GROUP + 2 * reach) * band, lanes), BF16),
        ],
    )
    terms = jnp.concatenate([terms[0], other_core(terms[1])], axis=0)
    gathered = exchange(terms.reshape(spots, band, LANES))
    gradient = call(
        functools.partial(collect_body, (probes, tiles, y_count, lat_count, window, columns)),
        shape(2, 2, band, columns, dtype=F32),
        [offsets],
        [gathered],
        (1_000_000, 2_000_000),
    )
    return gradient[:, None]


def solution(mesh):
    depth_count, lat_count = mesh.devices.shape
    grid = mesh.devices.reshape(depth_count // CORES, CORES, lat_count // GROUP, GROUP)
    fine = Mesh(grid, ("y", "core", "z", "x"))
    depth, lat = ("y", "core"), ("z", "x")
    in_specs = (
        P(None, depth, None, lat, None),
        P(None, None, lat, None),
        P(None, lat, None),
        P(),
        P(),
    )
    out_specs = P(None, depth, None, lat, None)
    return jax.shard_map(local, mesh=fine, in_specs=in_specs, out_specs=out_specs, check_vma=False)
```

```python
import functools

import jax
import jax.numpy as jnp
from jax import lax
from jax.experimental import pallas as pl
from jax.experimental.pallas import tpu as pltpu
from jax.sharding import Mesh
from jax.sharding import PartitionSpec as P

F32 = jnp.float32
BF16 = jnp.bfloat16
LANES = 128
PIECE = 64
CORES = 2
GROUP = 4
TAIL = 8
STRIP = 2
VMEM_BYTES = 16 * 1024 * 1024
WIDE_BYTES = 60 * 1024 * 1024


def vmem_spec():
    return pl.BlockSpec(memory_space=pltpu.VMEM)


def smem_spec():
    return pl.BlockSpec(memory_space=pltpu.SMEM)


def call(body, outs, scalars, arrays, cost, scratch=(), outside=0, grant=VMEM_BYTES):
    in_specs = [smem_spec()] * len(scalars)
    in_specs += [pl.BlockSpec(memory_space=pltpu.HBM)] * outside
    in_specs += [vmem_spec()] * (len(arrays) - outside)
    return pl.pallas_call(
        body,
        out_shape=outs,
        in_specs=in_specs,
        out_specs=jax.tree.map(lambda _: vmem_spec(), outs),
        scratch_shapes=list(scratch),
        compiler_params=pltpu.CompilerParams(vmem_limit_bytes=grant),
        cost_estimate=pl.CostEstimate(flops=cost[0], bytes_accessed=cost[1], transcendentals=0),
    )(*scalars, *arrays)


def tile_at(x, y, y_count, probes):
    rows = y_count // probes
    probe, row = y // rows, y % rows
    return probe, row * GROUP + (x if row % 2 == 0 else GROUP - 1 - x)


def tile_slots(y_count, probes, core):
    slots = {}
    for x in range(GROUP):
        base = lax.rem(x + core * (GROUP // CORES), GROUP) * y_count
        for y in range(y_count):
            slots[tile_at(x, y, y_count, probes)] = base + y
    return slots


def low_lanes(rows):
    return lax.broadcasted_iota(jnp.int32, (rows, LANES), 1) < PIECE


def swap_halves(cells):
    return pltpu.roll(cells, PIECE, 1)


def half_of(offsets, probe, band, lat, lat_count):
    first = offsets[probe, 0] // band
    return (first + lax.rem(lat - first + lat_count, lat_count)) // lat_count


def packed(real, imag, tiles):
    span = real.shape[1]
    real_on = pltpu.roll(real, span - PIECE, 1)
    imag_on = pltpu.roll(imag, span - PIECE, 1)
    low = low_lanes(real.shape[0])
    out = []
    for tile in range(tiles):
        base = tile // 2 * LANES
        here, there = slice(base, base + LANES), slice(base + LANES, base + 2 * LANES)
        if tile % 2 == 0:
            middle = jnp.where(low, real[:, there], imag_on[:, here])
            out.append((real[:, here], middle, imag[:, here]))
        else:
            middle = jnp.where(low, real_on[:, there], imag[:, there])
            out.append((real_on[:, here], middle, imag_on[:, here]))
    return out


def cos_sin(phase):
    half = 0.5 * phase
    square = half * half
    sin, cos = 1.0 / 6227020800.0, 1.0 / 479001600.0
    for term in (-39916800.0, 362880.0, -5040.0, 120.0, -6.0, 1.0):
        sin = sin * square + 1.0 / term
    for term in (-3628800.0, 40320.0, -720.0, 24.0, -2.0, 1.0):
        cos = cos * square + 1.0 / term
    sin = sin * half
    return 1.0 - 2.0 * (sin * sin), 2.0 * (sin * cos)


def prepare_body(
    dims, offsets, potential, incident, measured, sent, pot_buf, inc_buf, mea_buf, sems
):
    probes, tiles, halo, y_count, lat_count = dims
    band, columns = pot_buf.shape[2], pot_buf.shape[3]
    window = inc_buf.shape[3]
    span = window + 2 * halo
    y, core = lax.axis_index("y"), lax.axis_index("core")
    lat = lax.axis_index("z") * GROUP + lax.axis_index("x")
    row = (y * CORES + core) * STRIP
    first = pl.multiple_of(row // TAIL * TAIL, TAIL)
    copies = []
    for probe in range(probes):
        half = half_of(offsets, probe, band, lat, lat_count)
        copies.append(
            pltpu.make_async_copy(potential.at[:, half], pot_buf.at[probe], sems.at[probe])
        )
    copies.append(
        pltpu.make_async_copy(incident.at[:, :, pl.ds(first, TAIL)], inc_buf, sems.at[probes])
    )
    copies.append(
        pltpu.make_async_copy(measured.at[:, pl.ds(first, TAIL)], mea_buf, sems.at[probes + 1])
    )
    for copy in copies:
        copy.start()
    slots = tile_slots(y_count, probes, core)
    lane = lax.broadcasted_iota(jnp.int32, (band, span), 1)
    inside = (lane >= halo) & (lane < window + halo)
    for probe in range(probes):
        copies[probe].wait()
        turn = lax.rem(columns + halo - offsets[probe, 1], columns)
        phase = pltpu.roll(pot_buf[probe, 0], turn, 1)[:, :span]
        absorb = pltpu.roll(pot_buf[probe, 1], turn, 1)[:, :span]
        damping = jnp.where(inside, jnp.exp(-absorb), 0.0)
        cos, sin = cos_sin(phase)
        for tile, parts in enumerate(packed(damping * cos, damping * sin, tiles)):
            for at, part in enumerate(parts):
                rows = slice(at * band, (at + 1) * band)
                sent[slots[probe, tile], rows] = part.astype(BF16)
    copies[probes].wait()
    copies[probes + 1].wait()
    lift = lax.rem(first + TAIL - row, TAIL)
    rest = jnp.zeros((TAIL, 2 * halo), F32)
    place = lax.broadcasted_iota(jnp.int32, (TAIL, LANES), 0) // STRIP
    low = low_lanes(TAIL)
    for probe in range(probes):
        wide = []
        for part in range(2):
            rows = pltpu.roll(inc_buf[part, probe], lift, 0)
            wide.append(pltpu.roll(jnp.concatenate([rows, rest], axis=1), halo, 1))
        rows = pltpu.roll(pltpu.roll(mea_buf[probe], lift, 0), 3 * STRIP, 0)
        coarse = rows.astype(BF16).astype(F32)
        fine = rows - coarse
        coarse_on = pltpu.roll(coarse, window - PIECE, 1)
        fine_back = pltpu.roll(fine, PIECE, 1)
        for tile, parts in enumerate(packed(wide[0], wide[1], tiles)):
            here = slice(tile // 2 * LANES, tile // 2 * LANES + LANES)
            if tile % 2 == 0:
                cells = jnp.where(low, coarse[:, here], fine_back[:, here])
            else:
                cells = jnp.where(low, coarse_on[:, here], fine[:, here])
            for at, part in enumerate(parts):
                moved = pltpu.roll(part, at * STRIP, 0) if at else part
                cells = jnp.where(place == at, moved, cells)
            sent[slots[probe, tile], 3 * band :] = cells.astype(BF16)


def banded(taps, diff, half_width, conj):
    count = 2 * half_width + 1
    real = jnp.zeros(diff.shape, F32)
    imag = jnp.zeros(diff.shape, F32)
    for tap in range(count):
        hit = diff == tap - half_width
        source = count - 1 - tap if conj else tap
        real = jnp.where(hit, taps[source], real)
        value = taps[count + source]
        imag = jnp.where(hit, -value if conj else value, imag)
    return real, imag


def matrices_body(dims, conj, offsets, taps, *outs):
    band, half_width, y_count, probes, lat_count, reach, phase_rows = dims
    own = lax.axis_index("y") // (y_count // probes)
    start = lax.axis_index("z") * GROUP + lax.axis_index("core") * (GROUP // CORES) - reach
    base = lax.rem(start - offsets[own, 0] // band + 2 * lat_count, lat_count)

    def window_row(rows, axis):
        skip = (phase_rows[0] - rows) // 2
        index = lax.broadcasted_iota(jnp.int32, (rows, rows), axis) + skip
        at = index + base * band
        return jnp.where(at >= lat_count * band, at - lat_count * band, at)

    def column(lanes, axis):
        index = lax.broadcasted_iota(jnp.int32, (lanes, lanes), axis)
        return jnp.where(index >= LANES, index - LANES, index), index >= LANES

    count = len(phase_rows)
    for out, rows in zip(outs[:count], phase_rows):
        diff = window_row(rows, 1) - window_row(rows, 0)
        real, imag = banded(taps, diff, half_width, conj)
        out[...] = jnp.concatenate([real, imag], axis=1).astype(BF16)
    for out in outs[count:]:
        in_col, in_imag = column(out.shape[0], 0)
        out_col, out_imag = column(out.shape[0], 1)
        real, imag = banded(taps, in_col - out_col, half_width, conj)
        signed = jnp.where(in_imag, -imag, imag)
        out[...] = jnp.where(in_imag == out_imag, real, signed).astype(BF16)


def parts_of(cells):
    return tuple(cells[:, at : at + LANES] for at in range(0, cells.shape[1], LANES))


def band_rows(own, halo, band, core, index, of_other):
    reach = halo.shape[0] * band
    if index >= own.shape[0]:
        at = core * (reach + own.shape[0] * band) + (index - own.shape[0]) * band
    else:
        half = own.shape[0] // CORES
        later = core if (index < half) != of_other else CORES - 1 - core
        at = reach + (later * half + index % half) * band
    return pl.multiple_of(at, band)


def fill_layers(layers, sources, y, band, core):
    for of_other, (own, halo) in enumerate((sources[:2], sources[2:])):
        parity = CORES - 1 - core if of_other else core
        for index in range(own.shape[0] + halo.shape[0]):
            rows = pl.ds(band_rows(own, halo, band, core, index, bool(of_other)), band)
            inner = index - own.shape[0]
            cells = own[index, y, : 3 * band] if inner < 0 else halo[inner, y, : 3 * band]
            for at in range(3):
                cols = slice(at * LANES, (at + 1) * LANES)
                layers[CORES * y + parity, rows, cols] = cells[at * band : (at + 1) * band]


def two_tiles(packed_parts):
    first, middle, last = packed_parts
    low = low_lanes(first.shape[0])
    real = jnp.where(low, swap_halves(first), swap_halves(middle))
    return first, last, real, jnp.where(low, swap_halves(last), middle)


def one_tile(parts):
    low = low_lanes(parts[0].shape[0])
    on, back = LANES - PIECE // 2, PIECE // 2
    return tuple(
        jnp.where(low, pltpu.roll(parts[at], on, 1), pltpu.roll(parts[at + 2], back, 1))
        for at in range(2)
    )


def narrowed(packed_parts):
    first, middle, last = packed_parts
    edge = lax.broadcasted_iota(jnp.int32, first.shape, 1) < LANES - PIECE // 2
    on, back = LANES - PIECE // 2, PIECE // 2
    real = jnp.where(edge, pltpu.roll(first, on, 1), pltpu.roll(middle, on, 1))
    imag = jnp.where(edge, pltpu.roll(last, on, 1), pltpu.roll(middle, back, 1))
    return real, imag


def own_columns(parts, rows):
    lane = lax.broadcasted_iota(jnp.int32, (rows, LANES), 1)
    low = lane < PIECE
    if len(parts) == 4:
        real = jnp.where(lane < PIECE // 2, swap_halves(parts[0]), parts[2])
        imag = jnp.where(lane < PIECE + PIECE // 2, parts[1], swap_halves(parts[3]))
        return jnp.where(low, real, imag)
    real = pltpu.roll(parts[0], LANES - PIECE // 2, 1)
    return jnp.where(low, real, pltpu.roll(parts[1], PIECE // 2, 1))


def times(t, field, conj):
    sign = -1.0 if conj else 1.0
    out = []
    for at in range(0, len(t), 2):
        out.append(t[at] * field[at] - sign * (t[at + 1] * field[at + 1]))
        out.append(t[at] * field[at + 1] + sign * (t[at + 1] * field[at]))
    return tuple(out)


def along_rows(matrix, parts):
    crossed = []
    for at in range(0, len(parts), 2):
        crossed += [-parts[at + 1], parts[at]]
    both = [jnp.concatenate(rows, axis=1) for rows in (parts, crossed)]
    field = jnp.concatenate(both, axis=0).astype(BF16)
    return parts_of(jnp.dot(matrix, field, preferred_element_type=F32))


def along_cols(matrix, parts):
    rows = parts[0].shape[0]
    tiles = [jnp.concatenate(parts[at : at + 2], axis=1) for at in range(0, len(parts), 2)]
    field = jnp.concatenate(tiles, axis=0).astype(BF16)
    out = jnp.dot(field, matrix, preferred_element_type=F32)
    result = ()
    for at in range(len(tiles)):
        result += parts_of(out[at * rows : (at + 1) * rows])
    return result


def phases(dims):
    phase_rows, y_count = dims
    each = y_count // len(phase_rows)
    for at, rows in enumerate(phase_rows):
        skip = (phase_rows[0] - rows) // 2
        yield at, at * each, each, skip, rows, at < len(phase_rows) // 2


def layer_parts(layers, index, core, reach, skip, rows, wide):
    at = pl.multiple_of(core * reach + skip, 16)
    parts = parts_of(layers[index, pl.ds(at, rows)].astype(F32))
    return two_tiles(parts) if wide else narrowed(parts)


def forward_body(dims, *refs):
    band, phase_rows = dims
    count = len(phase_rows)
    row_mats, col_mat = refs[:count], refs[count]
    own, halo, o_own, o_halo, kept, seed, layers, goal, wave = refs[count + 1 :]
    sources = (own, halo, o_own, o_halo)
    core = lax.axis_index("core")
    total = phase_rows[0]
    own_rows = own.shape[0] * band // CORES
    head = (total - own_rows) // 2
    reach = halo.shape[0] * band
    y_count = own.shape[1]
    row = lax.broadcasted_iota(jnp.int32, (TAIL, LANES), 0)
    upper = row < TAIL // 2
    mine = lax.rem(row // STRIP, CORES) == core

    def both_strips(cells, o_cells):
        one = pltpu.roll(cells[3 * band :].astype(F32), STRIP * core, 0)
        two = pltpu.roll(o_cells[3 * band :].astype(F32), STRIP * (CORES - 1 - core), 0)
        return jnp.where(mine, one, two), jnp.where(mine, two, one)

    bands = own.shape[0] + halo.shape[0]
    for index in range(bands):
        base = band_rows(own, halo, band, core, index, False)
        for pair in range(y_count // 2):
            strips = []
            for y in (2 * pair, 2 * pair + 1):
                if index < own.shape[0]:
                    across = (index + own.shape[0] // CORES) % own.shape[0]
                    strips.append(both_strips(own[index, y], o_own[across, y]))
                else:
                    inner = index - own.shape[0]
                    strips.append(both_strips(halo[inner, y], o_halo[inner, y]))
            (even, even_mid), (odd, odd_mid) = strips
            rows = pl.ds(pl.multiple_of(base + pair * TAIL, TAIL), TAIL)
            turn = TAIL // 2
            wave[rows, :LANES] = jnp.where(upper, even, pltpu.roll(odd, turn, 0))
            wave[rows, LANES : 2 * LANES] = jnp.where(
                upper, pltpu.roll(even_mid, TAIL - STRIP, 0), pltpu.roll(odd_mid, STRIP, 0)
            )
            wave[rows, 2 * LANES :] = jnp.where(upper, pltpu.roll(even, turn, 0), odd)
            if index < own.shape[0] // CORES:
                both = jnp.where(
                    upper, pltpu.roll(even_mid, STRIP, 0), pltpu.roll(odd_mid, TAIL - STRIP, 0)
                )
                at = index * band + pair * TAIL
                goal[at : at + TAIL] = both + swap_halves(both)
    fill_layers(layers, sources, 0, band, core)
    psi = two_tiles(parts_of(wave[pl.ds(pl.multiple_of(core * reach, band), total)]))
    done = 0
    for phase, y_first, each, skip, rows, wide in phases((phase_rows, y_count)):
        mine_rows = slice(head - skip, head - skip + own_rows)
        psi = tuple(part[skip - done : skip - done + rows] for part in psi)
        done = skip
        if phase == count // 2:
            psi = one_tile(psi)
        for y in range(y_first, y_first + each):
            if y + 1 < y_count:
                fill_layers(layers, sources, y + 1, band, core)
            for parity in range(CORES):
                t = layer_parts(layers, CORES * y + parity, core, reach, skip, rows, wide)
                product = times(t, psi, False)
                inner = [part[mine_rows] for part in product]
                kept[CORES * y + parity] = own_columns(inner, own_rows).astype(BF16)
                spread = along_rows(row_mats[phase][...], product)
                psi = along_cols(col_mat[...], spread)
    wave_out = own_columns([part[head - done : head - done + own_rows] for part in psi], own_rows)
    square = wave_out * wave_out
    residual = square + swap_halves(square) - goal[...]
    seed[...] = (2.0 * residual * wave_out).astype(BF16)


def backward_body(dims, *refs):
    band, phase_rows = dims
    count = len(phase_rows)
    row_mats, col_mat = refs[:count], refs[count]
    own, halo, o_own, o_halo, kept, seeds, beside, beyond = refs[count + 1 : count + 9]
    terms, field, layers = refs[count + 9 :]
    sources = (own, halo, o_own, o_halo)
    core = lax.axis_index("core")
    own_rows = own.shape[0] * band // CORES
    head = (phase_rows[0] - own_rows) // 2
    reach = halo.shape[0] * band
    y_count = own.shape[1]
    low_own = low_lanes(own_rows)
    tail = phase_rows[0] - own_rows

    for part, base in ((seeds, head), (beside, (1 - core) * tail), (beyond, core * tail)):
        left, middle = part[0].astype(F32), part[1].astype(F32)
        rows = pl.ds(base if part is seeds else pl.multiple_of(base, band), own_rows)
        field[rows, :LANES] = jnp.where(low_own, left, swap_halves(middle)).astype(BF16)
        field[rows, LANES : 2 * LANES] = part[2]
        field[rows, 2 * LANES :] = jnp.where(low_own, swap_halves(left), middle).astype(BF16)

    fill_layers(layers, sources, y_count - 1, band, core)
    state = two_tiles(parts_of(field[...].astype(F32)))
    done = 0
    for phase, y_first, each, skip, rows, wide in phases((phase_rows, y_count)):
        mine_rows = slice(head - skip, head - skip + own_rows)
        state = tuple(part[skip - done : skip - done + rows] for part in state)
        done = skip
        if phase == count // 2:
            state = one_tile(state)
        for y in reversed(range(y_count - y_first - each, y_count - y_first)):
            if y > 0:
                fill_layers(layers, sources, y - 1, band, core)
            for parity in reversed(range(CORES)):
                spread = along_cols(col_mat[...], state)
                back = along_rows(row_mats[phase][...], spread)
                t = layer_parts(layers, CORES * y + parity, core, reach, skip, rows, wide)
                state = times(t, back, True)
                u = kept[CORES * y + parity].astype(F32)
                v = own_columns([part[mine_rows] for part in back], own_rows)
                u_turn, v_turn = swap_halves(u), swap_halves(v)
                phase_term = u * v_turn - u_turn * v
                term = jnp.where(low_own, phase_term, -(u * v + u_turn * v_turn)).astype(BF16)
                owner = lax.rem(core + parity, CORES)
                for index in range(terms.shape[1]):
                    terms[owner, index, y] = term[index * band : (index + 1) * band]


def collect_body(dims, offsets, terms, gradient):
    probes, tiles, y_count, lat_count, window, columns = dims
    band = terms.shape[1]
    lat = lax.axis_index("z") * GROUP + lax.axis_index("x")
    slots = tile_slots(y_count, probes, lax.axis_index("core"))
    low = low_lanes(band)
    rest = jnp.zeros((band, columns - window), F32)
    moved = []
    for probe in range(probes):
        parts = ([], [])
        for pair in range(tiles // 2):
            one = terms[slots[probe, 2 * pair]].astype(F32)
            two = terms[slots[probe, 2 * pair + 1]].astype(F32)
            parts[0].append(jnp.where(low, one, swap_halves(two)))
            parts[1].append(jnp.where(low, swap_halves(one), two))
        half = half_of(offsets, probe, band, lat, lat_count)
        for part in range(2):
            row = pltpu.roll(jnp.concatenate(parts[part] + [rest], axis=1), offsets[probe, 1], 1)
            moved.append((part, half, row))
    for part in range(2):
        for at in range(2):
            total = jnp.zeros((band, columns), F32)
            for which, half, row in moved:
                if which == part:
                    total = total + jnp.where(half == at, row, 0.0)
            gradient[part, at] = total


def local(potential, incident, measured, offsets, kernel):
    y_count = lax.axis_size("y")
    z_count = lax.axis_size("z")
    lat_count = z_count * GROUP
    band = potential.shape[3]
    columns = potential.shape[4]
    window = incident.shape[3]
    probes = incident.shape[1]
    half_width = (kernel.shape[1] - 1) // 2
    slices = y_count * CORES
    halo = slices * half_width
    tiles = y_count * GROUP // probes
    spots = y_count * GROUP
    reach = halo // band
    own_rows = GROUP // CORES * band
    phase_rows = tuple(own_rows + 2 * halo - at for at in range(0, 2 * halo, band))
    lanes = 3 * LANES
    taps = kernel.astype(F32).reshape(-1)
    core = lax.axis_index("core")

    def shape(*dims, dtype=BF16):
        return jax.ShapeDtypeStruct(dims, dtype)

    sent = call(
        functools.partial(prepare_body, (probes, tiles, halo, y_count, lat_count)),
        shape(spots, 3 * band + TAIL, LANES),
        [offsets],
        [potential[:, 0], incident, measured],
        (20_000_000, 3_000_000),
        [
            pltpu.VMEM((probes, 2, band, columns), F32),
            pltpu.VMEM((2, probes, TAIL, window), F32),
            pltpu.VMEM((probes, TAIL, window), F32),
            pltpu.SemaphoreType.DMA((probes + 2,)),
        ],
        outside=3,
        grant=WIDE_BYTES,
    )
    mat_shapes = tuple(shape(rows, 2 * rows) for rows in phase_rows)
    mat_shapes += (shape(2 * LANES, 2 * LANES),)
    mat_dims = (band, half_width, y_count, probes, lat_count, reach, phase_rows)

    def matrices(conj, taps):
        body = functools.partial(matrices_body, mat_dims, conj)
        return call(body, mat_shapes, [offsets, taps], [], (20_000_000, 700_000))

    def spot_of(z, at_core):
        return at_core * z_count + z % z_count

    steps_z = range(z_count)
    same = [(spot_of(i, 0), spot_of(i + 1, 0)) for i in steps_z]
    same += [(spot_of(i + 1, 1), spot_of(i, 1)) for i in steps_z]
    cross = [(spot_of(i, 1), spot_of(i + 1, 0)) for i in steps_z]
    cross += [(spot_of(i + 1, 0), spot_of(i, 1)) for i in steps_z]

    def other_core(cells):
        return lax.ppermute(cells, "core", [(i, CORES - 1 - i) for i in range(CORES)])

    groups = []
    for at_core in range(CORES):
        for z in range(z_count):
            order = [(x + at_core * (GROUP // CORES)) % GROUP for x in range(GROUP)]
            groups.append(
                [
                    ((y * CORES + at_core) * z_count + z) * GROUP + x
                    for x in order
                    for y in range(y_count)
                ]
            )

    def exchange(blocks):
        axes = ("y", "core", "z", "x")
        return lax.all_to_all(blocks, axes, 0, 0, axis_index_groups=groups, tiled=False)

    own = exchange(sent).reshape(GROUP, y_count, 3 * band + TAIL, LANES)
    edge = lax.ppermute(own[GROUP - reach :], ("core", "z"), same)
    o_edge = lax.ppermute(own[:reach], ("core", "z"), cross)
    o_own, tied_taps = lax.optimization_barrier((other_core(own), taps))
    edge, o_edge, *forward_mats = lax.optimization_barrier(
        (edge, o_edge, *matrices(False, tied_taps))
    )
    layers = (own, edge, o_own, o_edge)

    flops = slices * phase_rows[1] * lanes * (4 * phase_rows[1] + 2 * lanes)
    kept, seed = call(
        functools.partial(forward_body, (band, phase_rows)),
        (shape(slices, own_rows, LANES), shape(own_rows, LANES)),
        [],
        [*forward_mats, *layers],
        (flops, 6_000_000),
        [
            pltpu.VMEM((slices, (GROUP + 2 * reach) * band, lanes), BF16),
            pltpu.VMEM((own_rows, LANES), F32),
            pltpu.VMEM(((GROUP + 2 * reach) * band, lanes), F32),
        ],
    )
    at = {}
    for y in range(y_count):
        for x in range(GROUP):
            at[tile_at(x, y, y_count, probes)] = y * GROUP + x
    right = [(at[p, c], at[p, c + 1]) for p in range(probes) for c in range(tiles - 1)]
    seed, late_taps = lax.optimization_barrier((seed, taps))
    from_left = lax.ppermute(seed, ("y", "x"), right)
    from_right = lax.ppermute(seed, ("y", "x"), [(b, a) for a, b in right])
    from_left, from_right, *backward_mats = lax.optimization_barrier(
        (from_left, from_right, *matrices(True, late_taps))
    )
    seeds = jnp.stack([from_left, seed, from_right])
    beyond = lax.ppermute(seeds, ("core", "z"), cross)
    beside = other_core(seeds)
    terms = call(
        functools.partial(backward_body, (band, phase_rows)),
        shape(CORES, GROUP // CORES, y_count, band, LANES),
        [],
        [*backward_mats, *layers, kept, seeds, beside, beyond],
        (flops, 6_000_000),
        [
            pltpu.VMEM((phase_rows[0], lanes), BF16),
            pltpu.VMEM((slices, (GROUP + 2 * reach) * band, lanes), BF16),
        ],
    )
    terms = jnp.concatenate([terms[0], other_core(terms[1])], axis=0)
    gathered = exchange(terms.reshape(spots, band, LANES))
    gradient = call(
        functools.partial(collect_body, (probes, tiles, y_count, lat_count, window, columns)),
        shape(2, 2, band, columns, dtype=F32),
        [offsets],
        [gathered],
        (1_000_000, 2_000_000),
    )
    return gradient[:, None]


def solution(mesh):
    depth_count, lat_count = mesh.devices.shape
    grid = mesh.devices.reshape(depth_count // CORES, CORES, lat_count // GROUP, GROUP)
    fine = Mesh(grid, ("y", "core", "z", "x"))
    depth, lat = ("y", "core"), ("z", "x")
    in_specs = (
        P(None, depth, None, lat, None),
        P(None, None, lat, None),
        P(None, lat, None),
        P(),
        P(),
    )
    out_specs = P(None, depth, None, lat, None)
    return jax.shard_map(local, mesh=fine, in_specs=in_specs, out_specs=out_specs, check_vma=False)
```

```python
import functools

import jax
import jax.numpy as jnp
from jax import lax
from jax.experimental import pallas as pl
from jax.experimental.pallas import tpu as pltpu
from jax.sharding import Mesh
from jax.sharding import PartitionSpec as P

F32 = jnp.float32
BF16 = jnp.bfloat16
LANES = 128
PIECE = 64
CORES = 2
GROUP = 4
TAIL = 8
STRIP = 2
VMEM_BYTES = 16 * 1024 * 1024
WIDE_BYTES = 60 * 1024 * 1024


def vmem_spec():
    return pl.BlockSpec(memory_space=pltpu.VMEM)


def smem_spec():
    return pl.BlockSpec(memory_space=pltpu.SMEM)


def call(body, outs, scalars, arrays, cost, scratch=(), outside=0, grant=VMEM_BYTES):
    in_specs = [smem_spec()] * len(scalars)
    in_specs += [pl.BlockSpec(memory_space=pltpu.HBM)] * outside
    in_specs += [vmem_spec()] * (len(arrays) - outside)
    return pl.pallas_call(
        body,
        out_shape=outs,
        in_specs=in_specs,
        out_specs=jax.tree.map(lambda _: vmem_spec(), outs),
        scratch_shapes=list(scratch),
        compiler_params=pltpu.CompilerParams(vmem_limit_bytes=grant),
        cost_estimate=pl.CostEstimate(flops=cost[0], bytes_accessed=cost[1], transcendentals=0),
    )(*scalars, *arrays)


def tile_at(x, y, y_count, probes):
    rows = y_count // probes
    probe, row = y // rows, y % rows
    return probe, row * GROUP + (x if row % 2 == 0 else GROUP - 1 - x)


def tile_slots(y_count, probes, core):
    slots = {}
    for x in range(GROUP):
        base = lax.rem(x + core * (GROUP // CORES), GROUP) * y_count
        for y in range(y_count):
            slots[tile_at(x, y, y_count, probes)] = base + y
    return slots


def low_lanes(rows):
    return lax.broadcasted_iota(jnp.int32, (rows, LANES), 1) < PIECE


def swap_halves(cells):
    return pltpu.roll(cells, PIECE, 1)


def half_of(offsets, probe, band, lat, lat_count):
    first = offsets[probe, 0] // band
    return (first + lax.rem(lat - first + lat_count, lat_count)) // lat_count


def packed(real, imag, tiles):
    span = real.shape[1]
    real_on = pltpu.roll(real, span - PIECE, 1)
    imag_on = pltpu.roll(imag, span - PIECE, 1)
    low = low_lanes(real.shape[0])
    out = []
    for tile in range(tiles):
        base = tile // 2 * LANES
        here, there = slice(base, base + LANES), slice(base + LANES, base + 2 * LANES)
        if tile % 2 == 0:
            middle = jnp.where(low, real[:, there], imag_on[:, here])
            out.append((real[:, here], middle, imag[:, here]))
        else:
            middle = jnp.where(low, real_on[:, there], imag[:, there])
            out.append((real_on[:, here], middle, imag_on[:, here]))
    return out


def cos_sin(phase):
    half = 0.5 * phase
    square = half * half
    sin, cos = 1.0 / 6227020800.0, 1.0 / 479001600.0
    for term in (-39916800.0, 362880.0, -5040.0, 120.0, -6.0, 1.0):
        sin = sin * square + 1.0 / term
    for term in (-3628800.0, 40320.0, -720.0, 24.0, -2.0, 1.0):
        cos = cos * square + 1.0 / term
    sin = sin * half
    return 1.0 - 2.0 * (sin * sin), 2.0 * (sin * cos)


def prepare_body(
    dims, offsets, potential, incident, measured, sent, pot_buf, inc_buf, mea_buf, sems
):
    probes, tiles, halo, y_count, lat_count = dims
    band, columns = pot_buf.shape[2], potential.shape[3]
    window = inc_buf.shape[3]
    span = window + 2 * halo
    y, core = lax.axis_index("y"), lax.axis_index("core")
    lat = lax.axis_index("z") * GROUP + lax.axis_index("x")
    row = (y * CORES + core) * STRIP
    first = pl.multiple_of(row // TAIL * TAIL, TAIL)
    def first_column(probe):
        at = jnp.minimum(offsets[probe, 1] // LANES * LANES, columns - span)
        return pl.multiple_of(at, LANES)

    copies = []
    for probe in range(probes):
        half = half_of(offsets, probe, band, lat, lat_count)
        cut = potential.at[:, half, :, pl.ds(first_column(probe), span)]
        copies.append(pltpu.make_async_copy(cut, pot_buf.at[probe], sems.at[probe]))
    copies.append(
        pltpu.make_async_copy(incident.at[:, :, pl.ds(first, TAIL)], inc_buf, sems.at[probes])
    )
    copies.append(
        pltpu.make_async_copy(measured.at[:, pl.ds(first, TAIL)], mea_buf, sems.at[probes + 1])
    )
    for copy in copies:
        copy.start()
    slots = tile_slots(y_count, probes, core)
    lane = lax.broadcasted_iota(jnp.int32, (band, span), 1)
    inside = (lane >= halo) & (lane < window + halo)
    for probe in range(probes):
        copies[probe].wait()
        turn = lax.rem(span + halo - (offsets[probe, 1] - first_column(probe)), span)
        phase = pltpu.roll(pot_buf[probe, 0], turn, 1)
        absorb = pltpu.roll(pot_buf[probe, 1], turn, 1)
        damping = jnp.where(inside, jnp.exp(-absorb), 0.0)
        cos, sin = cos_sin(phase)
        for tile, parts in enumerate(packed(damping * cos, damping * sin, tiles)):
            for at, part in enumerate(parts):
                rows = slice(at * band, (at + 1) * band)
                sent[slots[probe, tile], rows] = part.astype(BF16)
    copies[probes].wait()
    copies[probes + 1].wait()
    lift = lax.rem(first + TAIL - row, TAIL)
    rest = jnp.zeros((TAIL, 2 * halo), F32)
    place = lax.broadcasted_iota(jnp.int32, (TAIL, LANES), 0) // STRIP
    low = low_lanes(TAIL)
    for probe in range(probes):
        wide = []
        for part in range(2):
            rows = pltpu.roll(inc_buf[part, probe], lift, 0)
            wide.append(pltpu.roll(jnp.concatenate([rows, rest], axis=1), halo, 1))
        rows = pltpu.roll(pltpu.roll(mea_buf[probe], lift, 0), 3 * STRIP, 0)
        coarse = rows.astype(BF16).astype(F32)
        fine = rows - coarse
        coarse_on = pltpu.roll(coarse, window - PIECE, 1)
        fine_back = pltpu.roll(fine, PIECE, 1)
        for tile, parts in enumerate(packed(wide[0], wide[1], tiles)):
            here = slice(tile // 2 * LANES, tile // 2 * LANES + LANES)
            if tile % 2 == 0:
                cells = jnp.where(low, coarse[:, here], fine_back[:, here])
            else:
                cells = jnp.where(low, coarse_on[:, here], fine[:, here])
            for at, part in enumerate(parts):
                moved = pltpu.roll(part, at * STRIP, 0) if at else part
                cells = jnp.where(place == at, moved, cells)
            sent[slots[probe, tile], 3 * band :] = cells.astype(BF16)


def banded(taps, diff, half_width, conj):
    count = 2 * half_width + 1
    real = jnp.zeros(diff.shape, F32)
    imag = jnp.zeros(diff.shape, F32)
    for tap in range(count):
        hit = diff == tap - half_width
        source = count - 1 - tap if conj else tap
        real = jnp.where(hit, taps[source], real)
        value = taps[count + source]
        imag = jnp.where(hit, -value if conj else value, imag)
    return real, imag


def matrices_body(dims, conj, offsets, taps, *outs):
    band, half_width, y_count, probes, lat_count, reach, phase_rows = dims
    own = lax.axis_index("y") // (y_count // probes)
    start = lax.axis_index("z") * GROUP + lax.axis_index("core") * (GROUP // CORES) - reach
    base = lax.rem(start - offsets[own, 0] // band + 2 * lat_count, lat_count)

    def window_row(shape, start, axis):
        at = lax.broadcasted_iota(jnp.int32, shape, axis) + start + base * band
        return jnp.where(at >= lat_count * band, at - lat_count * band, at)

    def column(lanes, axis):
        index = lax.broadcasted_iota(jnp.int32, (lanes, lanes), axis)
        return jnp.where(index >= LANES, index - LANES, index), index >= LANES

    count = len(phase_rows)
    for out, rows in zip(outs[:count], phase_rows):
        skip = (phase_rows[0] - rows) // 2
        for block, (start, end, first, last) in enumerate(row_blocks(rows)):
            size = (end - start, last - first)
            diff = window_row(size, first + skip, 1) - window_row(size, start + skip, 0)
            real, imag = banded(taps, diff, half_width, conj)
            out[block] = jnp.concatenate([real, imag], axis=1).astype(BF16)
    for out in outs[count:]:
        in_col, in_imag = column(out.shape[0], 0)
        out_col, out_imag = column(out.shape[0], 1)
        real, imag = banded(taps, in_col - out_col, half_width, conj)
        signed = jnp.where(in_imag, -imag, imag)
        out[...] = jnp.where(in_imag == out_imag, real, signed).astype(BF16)


def parts_of(cells):
    return tuple(cells[:, at : at + LANES] for at in range(0, cells.shape[1], LANES))


def band_rows(own, halo, band, core, index, of_other):
    reach = halo.shape[0] * band
    if index >= own.shape[0]:
        at = core * (reach + own.shape[0] * band) + (index - own.shape[0]) * band
    else:
        half = own.shape[0] // CORES
        later = core if (index < half) != of_other else CORES - 1 - core
        at = reach + (later * half + index % half) * band
    return pl.multiple_of(at, band)


def fill_layers(layers, sources, y, band, core):
    for of_other, (own, halo) in enumerate((sources[:2], sources[2:])):
        parity = CORES - 1 - core if of_other else core
        for index in range(own.shape[0] + halo.shape[0]):
            rows = pl.ds(band_rows(own, halo, band, core, index, bool(of_other)), band)
            inner = index - own.shape[0]
            cells = own[index, y, : 3 * band] if inner < 0 else halo[inner, y, : 3 * band]
            for at in range(3):
                cols = slice(at * LANES, (at + 1) * LANES)
                layers[CORES * y + parity, rows, cols] = cells[at * band : (at + 1) * band]


def two_tiles(packed_parts):
    first, middle, last = packed_parts
    low = low_lanes(first.shape[0])
    real = jnp.where(low, swap_halves(first), swap_halves(middle))
    return first, last, real, jnp.where(low, swap_halves(last), middle)


def one_tile(parts):
    low = low_lanes(parts[0].shape[0])
    on, back = LANES - PIECE // 2, PIECE // 2
    return tuple(
        jnp.where(low, pltpu.roll(parts[at], on, 1), pltpu.roll(parts[at + 2], back, 1))
        for at in range(2)
    )


def narrowed(packed_parts):
    first, middle, last = packed_parts
    edge = lax.broadcasted_iota(jnp.int32, first.shape, 1) < LANES - PIECE // 2
    on, back = LANES - PIECE // 2, PIECE // 2
    real = jnp.where(edge, pltpu.roll(first, on, 1), pltpu.roll(middle, on, 1))
    imag = jnp.where(edge, pltpu.roll(last, on, 1), pltpu.roll(middle, back, 1))
    return real, imag


def own_columns(parts, rows):
    lane = lax.broadcasted_iota(jnp.int32, (rows, LANES), 1)
    low = lane < PIECE
    if len(parts) == 4:
        real = jnp.where(lane < PIECE // 2, swap_halves(parts[0]), parts[2])
        imag = jnp.where(lane < PIECE + PIECE // 2, parts[1], swap_halves(parts[3]))
        return jnp.where(low, real, imag)
    real = pltpu.roll(parts[0], LANES - PIECE // 2, 1)
    return jnp.where(low, real, pltpu.roll(parts[1], PIECE // 2, 1))


def times(t, field, conj):
    sign = -1.0 if conj else 1.0
    out = []
    for at in range(0, len(t), 2):
        out.append(t[at] * field[at] - sign * (t[at + 1] * field[at + 1]))
        out.append(t[at] * field[at + 1] + sign * (t[at + 1] * field[at]))
    return tuple(out)


def row_blocks(rows):
    if rows <= LANES:
        return [(0, rows, 0, rows)]
    half, edge = rows // 2, 16
    return [(0, half, 0, half + edge), (half, rows, half - edge, rows)]


def along_rows(matrices, parts):
    crossed = []
    for at in range(0, len(parts), 2):
        crossed += [-parts[at + 1], parts[at]]
    both = [jnp.concatenate(rows, axis=1) for rows in (parts, crossed)]
    both = [cells.astype(BF16) for cells in both]
    out = []
    for block, (_, _, first, last) in enumerate(row_blocks(both[0].shape[0])):
        field = jnp.concatenate([cells[first:last] for cells in both], axis=0)
        out.append(jnp.dot(matrices[block], field, preferred_element_type=F32))
    return parts_of(jnp.concatenate(out, axis=0))


def along_cols(matrix, parts):
    rows = parts[0].shape[0]
    tiles = [jnp.concatenate(parts[at : at + 2], axis=1) for at in range(0, len(parts), 2)]
    field = jnp.concatenate(tiles, axis=0).astype(BF16)
    out = jnp.dot(field, matrix, preferred_element_type=F32)
    result = ()
    for at in range(len(tiles)):
        result += parts_of(out[at * rows : (at + 1) * rows])
    return result


def phases(dims):
    phase_rows, y_count = dims
    each = y_count // len(phase_rows)
    for at, rows in enumerate(phase_rows):
        skip = (phase_rows[0] - rows) // 2
        yield at, at * each, each, skip, rows, at < len(phase_rows) // 2


def layer_parts(layers, index, core, reach, skip, rows, wide):
    at = pl.multiple_of(core * reach + skip, 16)
    parts = parts_of(layers[index, pl.ds(at, rows)].astype(F32))
    return two_tiles(parts) if wide else narrowed(parts)


def forward_body(dims, *refs):
    band, phase_rows = dims
    count = len(phase_rows)
    row_mats, col_mat = refs[:count], refs[count]
    own, halo, o_own, o_halo, kept, seed, layers, goal, wave = refs[count + 1 :]
    sources = (own, halo, o_own, o_halo)
    core = lax.axis_index("core")
    total = phase_rows[0]
    own_rows = own.shape[0] * band // CORES
    head = (total - own_rows) // 2
    reach = halo.shape[0] * band
    y_count = own.shape[1]
    row = lax.broadcasted_iota(jnp.int32, (TAIL, LANES), 0)
    upper = row < TAIL // 2
    mine = lax.rem(row // STRIP, CORES) == core

    def both_strips(cells, o_cells):
        one = pltpu.roll(cells[3 * band :].astype(F32), STRIP * core, 0)
        two = pltpu.roll(o_cells[3 * band :].astype(F32), STRIP * (CORES - 1 - core), 0)
        return jnp.where(mine, one, two), jnp.where(mine, two, one)

    bands = own.shape[0] + halo.shape[0]
    for index in range(bands):
        base = band_rows(own, halo, band, core, index, False)
        for pair in range(y_count // 2):
            strips = []
            for y in (2 * pair, 2 * pair + 1):
                if index < own.shape[0]:
                    across = (index + own.shape[0] // CORES) % own.shape[0]
                    strips.append(both_strips(own[index, y], o_own[across, y]))
                else:
                    inner = index - own.shape[0]
                    strips.append(both_strips(halo[inner, y], o_halo[inner, y]))
            (even, even_mid), (odd, odd_mid) = strips
            rows = pl.ds(pl.multiple_of(base + pair * TAIL, TAIL), TAIL)
            turn = TAIL // 2
            wave[rows, :LANES] = jnp.where(upper, even, pltpu.roll(odd, turn, 0))
            wave[rows, LANES : 2 * LANES] = jnp.where(
                upper, pltpu.roll(even_mid, TAIL - STRIP, 0), pltpu.roll(odd_mid, STRIP, 0)
            )
            wave[rows, 2 * LANES :] = jnp.where(upper, pltpu.roll(even, turn, 0), odd)
            if index < own.shape[0] // CORES:
                both = jnp.where(
                    upper, pltpu.roll(even_mid, STRIP, 0), pltpu.roll(odd_mid, TAIL - STRIP, 0)
                )
                at = index * band + pair * TAIL
                goal[at : at + TAIL] = both + swap_halves(both)
    fill_layers(layers, sources, 0, band, core)
    psi = two_tiles(parts_of(wave[pl.ds(pl.multiple_of(core * reach, band), total)]))
    done = 0
    for phase, y_first, each, skip, rows, wide in phases((phase_rows, y_count)):
        mine_rows = slice(head - skip, head - skip + own_rows)
        psi = tuple(part[skip - done : skip - done + rows] for part in psi)
        done = skip
        if phase == count // 2:
            psi = one_tile(psi)
        for y in range(y_first, y_first + each):
            if y + 1 < y_count:
                fill_layers(layers, sources, y + 1, band, core)
            for parity in range(CORES):
                t = layer_parts(layers, CORES * y + parity, core, reach, skip, rows, wide)
                product = times(t, psi, False)
                inner = [part[mine_rows] for part in product]
                kept[CORES * y + parity] = own_columns(inner, own_rows).astype(BF16)
                spread = along_rows(row_mats[phase], product)
                psi = along_cols(col_mat[...], spread)
    wave_out = own_columns([part[head - done : head - done + own_rows] for part in psi], own_rows)
    square = wave_out * wave_out
    residual = square + swap_halves(square) - goal[...]
    seed[...] = (2.0 * residual * wave_out).astype(BF16)


def backward_body(dims, *refs):
    band, phase_rows = dims
    count = len(phase_rows)
    row_mats, col_mat = refs[:count], refs[count]
    own, halo, o_own, o_halo, kept, seeds, beside, beyond = refs[count + 1 : count + 9]
    terms, field, layers = refs[count + 9 :]
    sources = (own, halo, o_own, o_halo)
    core = lax.axis_index("core")
    own_rows = own.shape[0] * band // CORES
    head = (phase_rows[0] - own_rows) // 2
    reach = halo.shape[0] * band
    y_count = own.shape[1]
    low_own = low_lanes(own_rows)
    tail = phase_rows[0] - own_rows

    for part, base in ((seeds, head), (beside, (1 - core) * tail), (beyond, core * tail)):
        left, middle = part[0].astype(F32), part[1].astype(F32)
        rows = pl.ds(base if part is seeds else pl.multiple_of(base, band), own_rows)
        field[rows, :LANES] = jnp.where(low_own, left, swap_halves(middle)).astype(BF16)
        field[rows, LANES : 2 * LANES] = part[2]
        field[rows, 2 * LANES :] = jnp.where(low_own, swap_halves(left), middle).astype(BF16)

    fill_layers(layers, sources, y_count - 1, band, core)
    state = two_tiles(parts_of(field[...].astype(F32)))
    done = 0
    for phase, y_first, each, skip, rows, wide in phases((phase_rows, y_count)):
        mine_rows = slice(head - skip, head - skip + own_rows)
        state = tuple(part[skip - done : skip - done + rows] for part in state)
        done = skip
        if phase == count // 2:
            state = one_tile(state)
        for y in reversed(range(y_count - y_first - each, y_count - y_first)):
            if y > 0:
                fill_layers(layers, sources, y - 1, band, core)
            for parity in reversed(range(CORES)):
                spread = along_cols(col_mat[...], state)
                back = along_rows(row_mats[phase], spread)
                t = layer_parts(layers, CORES * y + parity, core, reach, skip, rows, wide)
                state = times(t, back, True)
                u = kept[CORES * y + parity].astype(F32)
                v = own_columns([part[mine_rows] for part in back], own_rows)
                u_turn, v_turn = swap_halves(u), swap_halves(v)
                phase_term = u * v_turn - u_turn * v
                term = jnp.where(low_own, phase_term, -(u * v + u_turn * v_turn)).astype(BF16)
                owner = lax.rem(core + parity, CORES)
                for index in range(terms.shape[1]):
                    terms[owner, index, y] = term[index * band : (index + 1) * band]


def collect_body(dims, offsets, terms, gradient):
    probes, tiles, y_count, lat_count, window, columns = dims
    band = terms.shape[1]
    lat = lax.axis_index("z") * GROUP + lax.axis_index("x")
    slots = tile_slots(y_count, probes, lax.axis_index("core"))
    low = low_lanes(band)
    rest = jnp.zeros((band, columns - window), F32)
    moved = []
    for probe in range(probes):
        parts = ([], [])
        for pair in range(tiles // 2):
            one = terms[slots[probe, 2 * pair]].astype(F32)
            two = terms[slots[probe, 2 * pair + 1]].astype(F32)
            parts[0].append(jnp.where(low, one, swap_halves(two)))
            parts[1].append(jnp.where(low, swap_halves(one), two))
        half = half_of(offsets, probe, band, lat, lat_count)
        for part in range(2):
            row = pltpu.roll(jnp.concatenate(parts[part] + [rest], axis=1), offsets[probe, 1], 1)
            moved.append((part, half, row))
    for part in range(2):
        for at in range(2):
            total = jnp.zeros((band, columns), F32)
            for which, half, row in moved:
                if which == part:
                    total = total + jnp.where(half == at, row, 0.0)
            gradient[part, at] = total


def local(potential, incident, measured, offsets, kernel):
    y_count = lax.axis_size("y")
    z_count = lax.axis_size("z")
    lat_count = z_count * GROUP
    band = potential.shape[3]
    columns = potential.shape[4]
    window = incident.shape[3]
    probes = incident.shape[1]
    half_width = (kernel.shape[1] - 1) // 2
    slices = y_count * CORES
    halo = slices * half_width
    tiles = y_count * GROUP // probes
    spots = y_count * GROUP
    reach = halo // band
    own_rows = GROUP // CORES * band
    phase_rows = tuple(own_rows + 2 * halo - at for at in range(0, 2 * halo, band))
    lanes = 3 * LANES
    taps = kernel.astype(F32).reshape(-1)
    core = lax.axis_index("core")

    def shape(*dims, dtype=BF16):
        return jax.ShapeDtypeStruct(dims, dtype)

    sent = call(
        functools.partial(prepare_body, (probes, tiles, halo, y_count, lat_count)),
        shape(spots, 3 * band + TAIL, LANES),
        [offsets],
        [potential[:, 0], incident, measured],
        (20_000_000, 3_000_000),
        [
            pltpu.VMEM((probes, 2, band, window + 2 * halo), F32),
            pltpu.VMEM((2, probes, TAIL, window), F32),
            pltpu.VMEM((probes, TAIL, window), F32),
            pltpu.SemaphoreType.DMA((probes + 2,)),
        ],
        outside=3,
        grant=WIDE_BYTES,
    )
    mat_shapes = ()
    for blocks in map(row_blocks, phase_rows):
        start, end, first, last = blocks[0]
        mat_shapes += (shape(len(blocks), end - start, 2 * (last - first)),)
    mat_shapes += (shape(2 * LANES, 2 * LANES),)
    mat_dims = (band, half_width, y_count, probes, lat_count, reach, phase_rows)

    def matrices(conj, taps):
        body = functools.partial(matrices_body, mat_dims, conj)
        return call(body, mat_shapes, [offsets, taps], [], (20_000_000, 700_000))

    def spot_of(z, at_core):
        return at_core * z_count + z % z_count

    steps_z = range(z_count)
    same = [(spot_of(i, 0), spot_of(i + 1, 0)) for i in steps_z]
    same += [(spot_of(i + 1, 1), spot_of(i, 1)) for i in steps_z]
    cross = [(spot_of(i, 1), spot_of(i + 1, 0)) for i in steps_z]
    cross += [(spot_of(i + 1, 0), spot_of(i, 1)) for i in steps_z]

    def other_core(cells):
        return lax.ppermute(cells, "core", [(i, CORES - 1 - i) for i in range(CORES)])

    groups = []
    for at_core in range(CORES):
        for z in range(z_count):
            order = [(x + at_core * (GROUP // CORES)) % GROUP for x in range(GROUP)]
            groups.append(
                [
                    ((y * CORES + at_core) * z_count + z) * GROUP + x
                    for x in order
                    for y in range(y_count)
                ]
            )

    def exchange(blocks):
        axes = ("y", "core", "z", "x")
        return lax.all_to_all(blocks, axes, 0, 0, axis_index_groups=groups, tiled=False)

    own = exchange(sent).reshape(GROUP, y_count, 3 * band + TAIL, LANES)
    edge = lax.ppermute(own[GROUP - reach :], ("core", "z"), same)
    o_edge = lax.ppermute(own[:reach], ("core", "z"), cross)
    o_own, tied_taps = lax.optimization_barrier((other_core(own), taps))
    edge, o_edge, *forward_mats = lax.optimization_barrier(
        (edge, o_edge, *matrices(False, tied_taps))
    )
    layers = (own, edge, o_own, o_edge)

    flops = slices * phase_rows[1] * lanes * (4 * phase_rows[1] + 2 * lanes)
    kept, seed = call(
        functools.partial(forward_body, (band, phase_rows)),
        (shape(slices, own_rows, LANES), shape(own_rows, LANES)),
        [],
        [*forward_mats, *layers],
        (flops, 6_000_000),
        [
            pltpu.VMEM((slices, (GROUP + 2 * reach) * band, lanes), BF16),
            pltpu.VMEM((own_rows, LANES), F32),
            pltpu.VMEM(((GROUP + 2 * reach) * band, lanes), F32),
        ],
    )
    at = {}
    for y in range(y_count):
        for x in range(GROUP):
            at[tile_at(x, y, y_count, probes)] = y * GROUP + x
    right = [(at[p, c], at[p, c + 1]) for p in range(probes) for c in range(tiles - 1)]
    seed, late_taps = lax.optimization_barrier((seed, taps))
    from_left = lax.ppermute(seed, ("y", "x"), right)
    from_right = lax.ppermute(seed, ("y", "x"), [(b, a) for a, b in right])
    from_left, from_right, *backward_mats = lax.optimization_barrier(
        (from_left, from_right, *matrices(True, late_taps))
    )
    seeds = jnp.stack([from_left, seed, from_right])
    beyond = lax.ppermute(seeds, ("core", "z"), cross)
    beside = other_core(seeds)
    terms = call(
        functools.partial(backward_body, (band, phase_rows)),
        shape(CORES, GROUP // CORES, y_count, band, LANES),
        [],
        [*backward_mats, *layers, kept, seeds, beside, beyond],
        (flops, 6_000_000),
        [
            pltpu.VMEM((phase_rows[0], lanes), BF16),
            pltpu.VMEM((slices, (GROUP + 2 * reach) * band, lanes), BF16),
        ],
    )
    terms = jnp.concatenate([terms[0], other_core(terms[1])], axis=0)
    gathered = exchange(terms.reshape(spots, band, LANES))
    gradient = call(
        functools.partial(collect_body, (probes, tiles, y_count, lat_count, window, columns)),
        shape(2, 2, band, columns, dtype=F32),
        [offsets],
        [gathered],
        (1_000_000, 2_000_000),
    )
    return gradient[:, None]


def solution(mesh):
    depth_count, lat_count = mesh.devices.shape
    grid = mesh.devices.reshape(depth_count // CORES, CORES, lat_count // GROUP, GROUP)
    fine = Mesh(grid, ("y", "core", "z", "x"))
    depth, lat = ("y", "core"), ("z", "x")
    in_specs = (
        P(None, depth, None, lat, None),
        P(None, None, lat, None),
        P(None, lat, None),
        P(),
        P(),
    )
    out_specs = P(None, depth, None, lat, None)
    return jax.shard_map(local, mesh=fine, in_specs=in_specs, out_specs=out_specs, check_vma=False)
```
